32 devices in a mesh: rep: 2 (over y), seq: 8 (over z, x), sub: 2 (over core).
Axes of the slice: x: 2, y: 2, z: 4, core: 2. Of those that a mesh axis runs over, the one named last changes fastest.
Arguments:
- lin_query: bfloat16 [2048, 2048], P(('rep', 'seq'), 'sub'), parts along dimension 0, may hold values from -6 to 6
- lin_key: bfloat16 [2048, 2048], P(('rep', 'seq'), 'sub'), parts along dimension 0, may hold values from -0.59765625 to 0.59765625
- lin_value: bfloat16 [2048, 2048], P(('rep', 'seq'), 'sub'), parts along dimension 0, may hold values from -6 to 6
- forget_log: float32 [2048, 16], P(('rep', 'seq'), 'sub'), parts along dimension 0, may hold values from -0.95 to 0
- norm_gain: float32 [2048], P('sub'), may hold values from 0.1 to 1.9
- soft_query: bfloat16 [2048, 2048], P(('rep', 'seq'), 'sub'), parts along dimension 0, may hold values from -34 to 34
- soft_key: bfloat16 [2048, 256], P(('rep', 'seq'), 'sub'), parts along dimension 0, may hold values from -6 to 6
- soft_value: bfloat16 [2048, 256], P(('rep', 'seq'), 'sub'), parts along dimension 0, may hold values from -6 to 6
- doc_lengths: int32 [2, 4], P('rep'), parts along dimension 0, may hold values from 1 to 512, 1024 in all within a row
Outputs:
- lin_out: bfloat16 [2048, 2048], P(('rep', 'seq'), 'sub'), parts along dimension 0
- soft_out: bfloat16 [2048, 2048], P(('rep', 'seq'), 'sub'), parts along dimension 0
The draws below stay inside these ranges and needn't reach their ends.
There are 2 independent parts, one for each index of `rep`. The reference program is written for one: setup_inputs(seed, part) draws one part's arguments, and reference() takes and returns one part's arrays. A program takes and returns all parts, laid end to end along the dimension named above; an argument that names none is the same for every part. Nothing has to cross between parts.
Inputs may be any that keep to these rules, and one draw needn't show every extreme that they name: `doc_lengths`: each row holds the lengths of one sequence's 4 documents in order; a row sums to 1024.
All inputs are finite; a program needn't handle non-finite values.
Results may differ from the reference program's by a relative error of at most 0.0075.
Values may be sent and summed in bfloat16 or wider, within the bound.
A program may use at most 192 MiB of HBM per device.

```python
import math
import jax
import jax.numpy as jnp
import numpy as np
from jax import lax

HEAD_COUNT = 16
KV_HEADS = 2
HEAD_DIM = 128
DOCS = 4
TOK_DEV = 128
SEQS = 1
SEQUENCE_LENGTH = 1024
TOKEN_TOTAL = 1024


def draw_forget_log(key, part):
    fast_share = 0.5
    kind_draw = jax.random.uniform(jax.random.fold_in(key, 101), (1, HEAD_COUNT))
    fast = kind_draw < fast_share
    fast_rate = jax.random.uniform(jax.random.fold_in(key, 102), (1, HEAD_COUNT), minval=1.0 / 50.0, maxval=1.0 / 30.0)
    slow_rate = jax.random.uniform(jax.random.fold_in(key, 103), (1, HEAD_COUNT), minval=0.3, maxval=1.0) * (math.log(10.0) / (2.0 * SEQUENCE_LENGTH))
    decay_speed = jnp.where(fast, fast_rate, slow_rate)
    blocks = TOKEN_TOTAL // TOK_DEV
    device_multiplier = jnp.exp(jax.random.uniform(jax.random.fold_in(key, 104), (blocks, 1, HEAD_COUNT), minval=math.log(0.5), maxval=math.log(2.0)))
    device_multiplier = jnp.broadcast_to(device_multiplier, (blocks, TOK_DEV, HEAD_COUNT)).reshape(TOKEN_TOTAL, HEAD_COUNT)
    coarse_estimate = jax.random.uniform(jax.random.fold_in(key, 105), (TOKEN_TOTAL, HEAD_COUNT), minval=0.5, maxval=1.5)
    spike_amount = jax.random.uniform(jax.random.fold_in(key, 106), (TOKEN_TOTAL, HEAD_COUNT)) < 3.0 / SEQUENCE_LENGTH
    spike_logarithm = jnp.log(jax.random.uniform(jax.random.fold_in(key, 107), (TOKEN_TOTAL, HEAD_COUNT), minval=0.45, maxval=0.8))
    return (-(decay_speed * device_multiplier * coarse_estimate) + jnp.where(spike_amount, spike_logarithm, 0.0)).astype(jnp.float32)


def query_key_pair(key):
    query_key = jax.random.fold_in(key, 201)
    key_key = jax.random.fold_in(key, 202)
    queries = jnp.clip(jax.random.normal(query_key, (TOKEN_TOTAL, HEAD_COUNT * HEAD_DIM)), -6.0, 6.0)
    keys = jnp.clip(jax.random.normal(key_key, (TOKEN_TOTAL, KV_HEADS * HEAD_DIM)), -6.0, 6.0)
    return (queries.astype(jnp.float32), keys.astype(jnp.float32))


def draw_soft_query(key, part):
    return query_key_pair(key)[0].astype(jnp.bfloat16)


def draw_soft_key(key, part):
    return query_key_pair(key)[1].astype(jnp.bfloat16)


def level_of(key, extent, split, least, high):
    gain, own = 1.0, jax.random.fold_in(key, 6)
    for axis_at, shards_of in split:
        steps = jnp.exp(jax.random.uniform(jax.random.fold_in(own, axis_at), (shards_of,), jnp.float32, least / len(split), high / len(split)))
        gain = gain * jnp.repeat(steps, extent[axis_at] // shards_of).reshape([-1 if axis == axis_at else 1 for axis in range(len(extent))])
    return gain


def profile(amount, total, bound, lean):
    portions = [(1 << 20) // math.isqrt(rank ** lean) + 1 for rank in range(2, amount + 1)]
    surplus, holding = total - bound - (amount - 1), [1] * (amount - 1)
    while surplus > 0:
        candidates = [i for i in range(amount - 1) if holding[i] < bound]
        pool, left = sum([portions[i] for i in candidates]), surplus
        for i in candidates:
            addition = min(bound - holding[i], max(1, left * portions[i] // pool), surplus)
            holding[i] = holding[i] + addition
            surplus = surplus - addition
    return np.array([bound] + holding)


def uneven(rng, count, total, limit, slope):
    if count == 2:
        one = jax.random.randint(rng, (), max(1, total - limit), min(limit, total - 1) + 1)
        return jnp.stack([one, total - one])
    tallies = jnp.asarray(profile(count, total, limit, slope), jnp.int32)
    couples = (count - 1) // 2
    donor, taker = tallies[1:1 + 2 * couples:2], tallies[2:2 + 2 * couples:2]
    slack = jnp.minimum(donor - 1, limit - taker)
    moved = jax.random.randint(jax.random.fold_in(rng, 1), (couples,), 0, 1 << 20) % (slack + 1)
    tallies = tallies.at[1:1 + 2 * couples:2].set(donor - moved).at[2:2 + 2 * couples:2].set(taker + moved)
    return tallies[jax.random.permutation(jax.random.fold_in(rng, 2), count)]


def noise(rng, extent, deviation, bound, cuts=(), kind=jnp.bfloat16):
    array = deviation * jax.random.normal(rng, extent, jnp.float32)
    if cuts:
        array = array * level_of(rng, extent, cuts, -0.22, 0.18)
    return jnp.clip(array, -bound, bound).astype(kind)


def setup_inputs(seed: int = 0, part: int = 0) -> dict:
    splits = jax.random.split(jax.random.key(seed), 10)
    part_keys = jax.random.split(jax.random.fold_in(splits[9], part), 10)
    return {
        "lin_query": noise(part_keys[0], (TOKEN_TOTAL, HEAD_COUNT * HEAD_DIM), 1.0, 6.0, ((0, 8), (1, 2))),
        "lin_key": noise(part_keys[1], (TOKEN_TOTAL, HEAD_COUNT * HEAD_DIM), 0.1, 0.59765625, ((0, 8), (1, 2))),
        "lin_value": noise(part_keys[2], (TOKEN_TOTAL, HEAD_COUNT * HEAD_DIM), 1.0, 6.0, ((0, 8), (1, 2))),
        "forget_log": draw_forget_log(jax.random.fold_in(jax.random.fold_in(splits[9], part), 71), part),
        "norm_gain": jnp.clip(1.0 + 0.18 * jax.random.normal(splits[4], (HEAD_COUNT * HEAD_DIM,), jnp.float32), 0.1, 1.9),
        "soft_query": draw_soft_query(jax.random.fold_in(jax.random.fold_in(splits[9], part), 71), part),
        "soft_key": draw_soft_key(jax.random.fold_in(jax.random.fold_in(splits[9], part), 71), part),
        "soft_value": noise(part_keys[7], (TOKEN_TOTAL, KV_HEADS * HEAD_DIM), 1.0, 6.0, ((0, 8), (1, 2))),
        "doc_lengths": jax.vmap(lambda own: uneven(own, DOCS, SEQUENCE_LENGTH, SEQUENCE_LENGTH // 2, 2))(jax.random.split(part_keys[8], SEQS)).reshape((SEQS, DOCS)).astype(jnp.int32),
    }


def document_table(doc_lengths):
    starts = jnp.cumsum(doc_lengths, axis=1) - doc_lengths
    where_at = jnp.arange(SEQUENCE_LENGTH, dtype=jnp.int32)
    ids = lax.optimization_barrier(jnp.sum((starts[:, None, :] <= where_at[None, :, None]).astype(jnp.int32), axis=2)) - 1
    ids = ids + (jnp.arange(SEQS, dtype=jnp.int32) * DOCS)[:, None]
    begins = jnp.any(starts[:, None, :] == where_at[None, :, None], axis=2)
    return (ids.reshape(TOKEN_TOTAL).astype(jnp.int32), begins.reshape(TOKEN_TOTAL))

def rounded(values):
    return lax.optimization_barrier(values.astype(jnp.bfloat16)).astype(jnp.float32)

def linear_block(state, pieces):
    queries, keys, values, forget, ids, begins = pieces
    cum = jnp.cumsum(forget, axis=0)
    live = (jnp.cumsum(begins.astype(jnp.int32)) == 0).astype(jnp.float32)
    order = jnp.arange(TOK_DEV, dtype=jnp.int32)
    mask = (ids[:, None] == ids[None, :]) & (order[None, :] <= order[:, None])
    diff = cum.T[:, :, None] - cum.T[:, None, :]
    decay = jnp.where(mask[None], jnp.exp(jnp.where(mask[None], diff, 0.0)), 0.0)
    queries_f = queries.astype(jnp.float32)
    keys_f = keys.astype(jnp.float32)
    values_f = values.astype(jnp.float32)
    scores = jnp.einsum('thd,shd->hts', queries_f, keys_f)
    weights = rounded(scores * decay)
    intra = jnp.einsum('hts,shd->thd', weights, values_f)
    tail_mask = ids == ids[-1]
    tail = jnp.where(tail_mask[:, None], jnp.exp(jnp.where(tail_mask[:, None], cum[-1][None, :] - cum, 0.0)), 0.0)
    keyed = rounded(keys_f * tail[:, :, None])
    local = jnp.einsum('shd,she->hde', keyed, values_f)
    carry = jnp.exp(cum[-1]) * live[-1]
    queried = rounded(queries_f * (jnp.exp(cum) * live[:, None])[:, :, None])
    inter = jnp.einsum('thd,hde->the', queried, rounded(state))
    new_state = carry[:, None, None] * state + local
    return (new_state, intra + inter)

def soft_head(queries, keys, values, mask):
    scores = jnp.dot(queries, keys.T, preferred_element_type=jnp.float32) * (1.0 / math.sqrt(HEAD_DIM))
    peak = lax.optimization_barrier(jnp.max(jnp.where(mask, scores, -jnp.inf), axis=1))
    weights = jnp.where(mask, jnp.exp(jnp.where(mask, scores - peak[:, None], 0.0)), 0.0)
    total = lax.optimization_barrier(jnp.sum(weights, axis=1))
    numer = jnp.dot(weights.astype(jnp.bfloat16), values, preferred_element_type=jnp.float32)
    return (numer / total[:, None]).astype(jnp.bfloat16)

def reference(lin_query, lin_key, lin_value, forget_log, norm_gain, soft_query, soft_key, soft_value, doc_lengths):
    ids, begins = document_table(doc_lengths)
    blocks = TOKEN_TOTAL // TOK_DEV
    shape_blocks = (blocks, TOK_DEV, HEAD_COUNT, HEAD_DIM)
    pieces = (lin_query.reshape(shape_blocks), lin_key.reshape(shape_blocks), lin_value.reshape(shape_blocks), forget_log.reshape(blocks, TOK_DEV, HEAD_COUNT), ids.reshape(blocks, TOK_DEV), begins.reshape(blocks, TOK_DEV))
    start_state = jnp.zeros((HEAD_COUNT, HEAD_DIM, HEAD_DIM), jnp.float32)
    unused, lin_sum = lax.scan(linear_block, start_state, pieces)
    lin_sum = lin_sum.reshape(TOKEN_TOTAL, HEAD_COUNT, HEAD_DIM)
    mean_square = lax.optimization_barrier(jnp.mean(lin_sum * lin_sum, axis=-1, keepdims=True))
    normed = lin_sum * lax.rsqrt(mean_square + 1e-06) * norm_gain.reshape(HEAD_COUNT, HEAD_DIM)
    lin_out = normed.reshape(TOKEN_TOTAL, HEAD_COUNT * HEAD_DIM).astype(jnp.bfloat16)
    group = HEAD_COUNT // KV_HEADS
    query_all = soft_query.reshape(SEQS, SEQUENCE_LENGTH, KV_HEADS, group, HEAD_DIM).transpose(0, 2, 3, 1, 4)
    key_all = soft_key.reshape(SEQS, SEQUENCE_LENGTH, KV_HEADS, HEAD_DIM).transpose(0, 2, 1, 3)
    value_all = soft_value.reshape(SEQS, SEQUENCE_LENGTH, KV_HEADS, HEAD_DIM).transpose(0, 2, 1, 3)
    ids_all = ids.reshape(SEQS, SEQUENCE_LENGTH)
    order = jnp.arange(SEQUENCE_LENGTH, dtype=jnp.int32)
    block_count = SEQUENCE_LENGTH // TOK_DEV
    block_order = jnp.arange(block_count, dtype=jnp.int32)
    inside = jnp.arange(TOK_DEV, dtype=jnp.int32)

    def one_sequence(items):
        queries, keys, values, seq_ids = items

        def one_kv(kv_items):
            kv_queries, kv_keys, kv_values = kv_items

            def one_head(head_queries):
                query_blocks = head_queries.reshape(block_count, TOK_DEV, HEAD_DIM)

                def one_block(block_items):
                    block_queries, block_index = block_items
                    first = (block_index * TOK_DEV).astype(jnp.int32)
                    rows = first + inside
                    row_ids = lax.dynamic_slice_in_dim(seq_ids, first, TOK_DEV, 0)
                    mask = (row_ids[:, None] == seq_ids[None, :]) & (order[None, :] <= rows[:, None])
                    return soft_head(block_queries, kv_keys, kv_values, mask)
                return lax.map(one_block, (query_blocks, block_order)).reshape(SEQUENCE_LENGTH, HEAD_DIM)
            return lax.map(one_head, kv_queries)
        return lax.map(one_kv, (queries, keys, values))
    soft = lax.map(one_sequence, (query_all, key_all, value_all, ids_all))
    soft_out = soft.transpose(0, 3, 1, 2, 4).reshape(TOKEN_TOTAL, HEAD_COUNT * HEAD_DIM)
    return (lin_out, soft_out)
```

```python
import functools
import math

import jax
import jax.numpy as jnp
from jax import lax
from jax.experimental import pallas as pl
from jax.experimental.pallas import tpu as pltpu
from jax.sharding import PartitionSpec as P

HEAD_DIM = 128


NEGATIVE = -1e30


def entering(array, axis, combine, identity):
    size, mine = (lax.axis_size(axis), lax.axis_index(axis))
    everything = jax.tree.map(
        lambda part, kind: lax.all_gather(part.astype(kind), axis),
        array,
        (jnp.bfloat16, jnp.bfloat16),
    )
    start = jax.tree.map(
        lambda part, zero: jnp.broadcast_to(jnp.asarray(zero, part.dtype), part.shape),
        array,
        identity,
    )

    def step(k, before):
        reached = k < mine
        new = combine(
            before, jax.tree.map(lambda part, own: part[k].astype(own.dtype), everything, array)
        )
        return jax.tree.map(lambda a, b: jnp.where(reached, a, b), new, before)

    return lax.fori_loop(0, size, step, start)


def passed_along(block, axis, distance):
    devices = range(lax.axis_size(axis))
    route = [(i - distance, i) for i in devices if i - distance in devices]
    return lax.ppermute(block, axis, route)


def document_ids(lengths_row, where_at):
    starts = jnp.cumsum(lengths_row) - lengths_row
    ids = jnp.sum((starts[None, :] <= where_at[:, None]).astype(jnp.int32), axis=1) - 1
    begins = jnp.any(starts[None, :] == where_at[:, None], axis=1)
    return (ids, begins)


def linear_parts(lin_query, lin_key, lin_value, forget_log, ids, begins):
    rows_here, heads_here = forget_log.shape
    queries = lin_query.reshape(rows_here, heads_here, HEAD_DIM)
    keys = lin_key.reshape(rows_here, heads_here, HEAD_DIM)
    values = lin_value.reshape(rows_here, heads_here, HEAD_DIM)
    cum = jnp.cumsum(forget_log, axis=0)
    live = (jnp.cumsum(begins.astype(jnp.int32)) == 0).astype(jnp.float32)
    order = jnp.arange(rows_here, dtype=jnp.int32)
    mask = (ids[:, None] == ids[None, :]) & (order[None, :] <= order[:, None])
    diff = cum.T[:, :, None] - cum.T[:, None, :]
    decay = jnp.where(mask[None], jnp.exp(jnp.where(mask[None], diff, 0.0)), 0.0)
    scores = jnp.einsum("thd,shd->hts", queries, keys, preferred_element_type=jnp.float32)
    weights = (scores * decay).astype(jnp.bfloat16)
    intra = jnp.einsum("hts,shd->thd", weights, values, preferred_element_type=jnp.float32)
    tail_mask = ids == ids[-1]
    tail = jnp.where(
        tail_mask[:, None], jnp.exp(jnp.where(tail_mask[:, None], cum[-1][None, :] - cum, 0.0)), 0.0
    )
    keyed = (keys * tail[:, :, None]).astype(jnp.bfloat16)
    local_state = jnp.einsum("shd,she->hde", keyed, values, preferred_element_type=jnp.float32)
    block_decay = jnp.exp(cum[-1]) * live[-1]
    queried = (queries * (jnp.exp(cum) * live[:, None])[:, :, None]).astype(jnp.bfloat16)
    return (intra, queried, local_state, block_decay)


def linear_finish(intra, queried, incoming, norm_gain):
    rows_here, heads_here, width = intra.shape
    inter = jnp.einsum(
        "thd,hde->the", queried, incoming.astype(jnp.bfloat16), preferred_element_type=jnp.float32
    )
    summed = intra + inter
    mean_square = jnp.mean(summed * summed, axis=-1, keepdims=True)
    normed = summed * lax.rsqrt(mean_square + 1e-06) * norm_gain.reshape(heads_here, width)
    return normed.reshape(rows_here, heads_here * width).astype(jnp.bfloat16)


def attend(running, queries, key_block, value_block, mask):
    peak, total, accum = running
    width = queries.shape[-1]
    scores = jnp.einsum(
        "tkgd,skd->kgts", queries, key_block, preferred_element_type=jnp.float32
    ) * (1.0 / math.sqrt(width))
    scores = jnp.where(mask, scores, NEGATIVE)
    new_peak = jnp.maximum(peak, jnp.max(scores, axis=-1))
    weights = jnp.where(mask, jnp.exp(scores - new_peak[..., None]), 0.0)
    rescale = jnp.exp(peak - new_peak)
    total = total * rescale + jnp.sum(weights, axis=-1)
    accum = accum * rescale[..., None] + jnp.einsum(
        "kgts,skd->kgtd",
        weights.astype(jnp.bfloat16),
        value_block,
        preferred_element_type=jnp.float32,
    )
    return (new_peak, total, accum)


def start_running(kv_here, group, count):
    return (
        jnp.full((kv_here, group, count), NEGATIVE, jnp.float32),
        jnp.zeros((kv_here, group, count), jnp.float32),
        jnp.zeros((kv_here, group, count, HEAD_DIM), jnp.float32),
    )


def finish_running(running, count, heads_here):
    peak, total, accum = running
    soft = (accum / total[..., None]).astype(jnp.bfloat16)
    return soft.transpose(2, 0, 1, 3).reshape(count, heads_here * HEAD_DIM)


def per_device(
    lin_query,
    lin_key,
    lin_value,
    forget_log,
    norm_gain,
    soft_query,
    soft_key,
    soft_value,
    doc_lengths,
):
    rows_here = lin_query.shape[0]
    seq_count = doc_lengths.shape[0]
    span = lax.axis_size("seq") // seq_count
    position = lax.axis_index("seq")
    rank = position % span
    lengths_row = doc_lengths[0]
    order = jnp.arange(rows_here, dtype=jnp.int32)
    query_where = rank * rows_here + order
    ids, begins = document_ids(lengths_row, query_where)
    intra, queried, local_state, block_decay = linear_parts(
        lin_query, lin_key, lin_value, forget_log, ids, begins
    )

    def combine_states(earlier, later):
        return (earlier[0] * later[0], later[0][:, None, None] * earlier[1] + later[1])

    identity = (jnp.ones_like(block_decay), jnp.zeros_like(local_state))
    scanned = entering((block_decay, local_state), "seq", combine_states, identity)
    lin_out = linear_finish(intra, queried, scanned[1], norm_gain)
    kv_here = soft_key.shape[1] // HEAD_DIM
    heads_here = soft_query.shape[1] // HEAD_DIM
    group = heads_here // kv_here
    queries = soft_query.reshape(rows_here, kv_here, group, HEAD_DIM)

    def piece_mask(start, count):
        key_where = start + jnp.arange(count, dtype=jnp.int32)
        source_ids, unused = document_ids(lengths_row, key_where)
        return (ids[:, None] == source_ids[None, :]) & (key_where[None, :] <= query_where[:, None])

    def attend_piece(running, key_piece, value_piece, start):
        count = key_piece.shape[0]
        key_block = key_piece.reshape(count, kv_here, HEAD_DIM)
        value_block = value_piece.reshape(count, kv_here, HEAD_DIM)
        return attend(running, queries, key_block, value_block, piece_mask(start, count))

    own_pair = jnp.stack([soft_key, soft_value])
    running = attend_piece(
        start_running(kv_here, group, rows_here), soft_key, soft_value, rank * rows_here
    )

    def visit_cycle(turn, state):
        moving, inner_state = state
        moving = passed_along(moving, "seq", 1)
        source = rank - turn - 1
        inner_state = lax.cond(
            source >= 0,
            lambda inner: attend_piece(inner, moving[0], moving[1], source * rows_here),
            lambda inner: inner,
            inner_state,
        )
        return (moving, inner_state)

    unused_pair, running = lax.fori_loop(0, span - 1, visit_cycle, (own_pair, running))
    soft_out = finish_running(running, rows_here, heads_here)
    return (lin_out, soft_out)


def block_kernel(
    span,
    heads,
    lens,
    lin_q,
    lin_k,
    lin_v,
    forget,
    gain,
    soft_q,
    soft_k,
    soft_v,
    lin_out,
    soft_out,
    keys,
    values,
    bias,
    local,
    packed,
    paired,
    carries,
    carries_in,
    arrived,
    onward,
    across,
    incoming,
    intra,
    queried,
    send_kv,
    recv_kv,
    send_pair,
    recv_pair,
    send_carry,
    recv_carry,
    send_chain,
    recv_chain,
    send_state,
    recv_state,
):
    f32, bf16 = jnp.float32, jnp.bfloat16
    rows = lin_q.shape[0]
    width = HEAD_DIM
    half = heads // 2
    window = span // 2
    me = lax.axis_index("seq")
    z, x = me // 2, me % 2
    other = me + 1 - 2 * x
    mesh_id = pl.DeviceIdType.MESH

    barrier = pltpu.get_barrier_semaphore()
    for d in range(1, window + 1):
        for target, ok in ((me + d, me + d < span), (me - d, me >= d)):

            @pl.when(ok)
            def _():
                pl.semaphore_signal(
                    barrier, inc=1, device_id={"seq": target}, device_id_type=mesh_id
                )

    def remote(src, dst, send, recv, target):
        return pltpu.make_async_remote_copy(
            src_ref=src,
            dst_ref=dst,
            send_sem=send,
            recv_sem=recv,
            device_id={"seq": target},
            device_id_type=mesh_id,
        )

    def kv_copy(d, which):
        src, dst = ((soft_k, keys), (soft_v, values))[which]
        return remote(
            src,
            dst.at[pl.ds(d * rows, rows)],
            send_kv.at[2 * d - 2 + which],
            recv_kv.at[2 * d - 2 + which],
            me + d,
        )

    def pair_copy(i):
        return remote(
            packed.at[half * (1 - x) + i], paired.at[i], send_pair.at[i], recv_pair.at[i], other
        )

    def carry_copy():
        return remote(carries, carries_in, send_carry, recv_carry, other)

    def chain_copy(i):
        return remote(onward.at[i], arrived.at[i], send_chain.at[i], recv_chain.at[i], me + 2)

    def state_copy(i):
        return remote(
            across.at[i], incoming.at[half * x + i], send_state.at[i], recv_state.at[i], other
        )

    first = me * rows
    starts = [jnp.int32(0)]
    for i in range(lens.shape[1] - 1):
        starts.append(starts[-1] + lens[0, i])
    where_col = first + lax.broadcasted_iota(jnp.int32, (rows, 1), 0)
    doc_col = jnp.zeros((rows, 1), jnp.int32)
    live_col = jnp.ones((rows, 1), f32)
    last = first + rows - 1
    doc_last = jnp.int32(0)
    live_last = jnp.float32(1.0)
    for s in starts:
        doc_col = jnp.maximum(doc_col, jnp.where(where_col >= s, s, 0))
        live_col = jnp.where((where_col >= s) & (s >= first), 0.0, live_col)
        doc_last = jnp.maximum(doc_last, jnp.where(last >= s, s, 0))
        live_last = jnp.where((last >= s) & (s >= first), 0.0, live_last)

    t_at = lax.broadcasted_iota(jnp.int32, (rows, rows), 0)
    s_at = lax.broadcasted_iota(jnp.int32, (rows, rows), 1)
    tri = (s_at <= t_at).astype(f32)
    logs = forget[...]
    cum = lax.dot_general(
        tri, logs, (((1,), (0,)), ((), ())), precision=lax.Precision.HIGHEST,
        preferred_element_type=f32,
    )
    cum_rows = lax.dot_general(
        logs, tri, (((0,), (1,)), ((), ())), precision=lax.Precision.HIGHEST,
        preferred_element_type=f32,
    )
    end = cum[rows - 1 : rows, :]
    tail_mask = where_col >= doc_last
    tail = jnp.where(tail_mask, jnp.exp(jnp.where(tail_mask, end - cum, 0.0)), 0.0)
    entry = jnp.exp(cum) * live_col
    carries[...] = jnp.broadcast_to(jnp.exp(cum_rows[:, rows - 1 : rows]) * live_last, carries.shape)

    def head(ref, h):
        return ref[:, h * width : (h + 1) * width]

    for h in range(heads):
        keyed = (head(lin_k, h).astype(f32) * tail[:, h : h + 1]).astype(bf16)
        state = lax.dot_general(
            keyed, head(lin_v, h), (((0,), (0,)), ((), ())), preferred_element_type=f32
        )
        local[h] = state
        packed[h] = state.astype(bf16)

    peers = jnp.minimum(me, window) + jnp.minimum(span - 1 - me, window)
    pl.semaphore_wait(barrier, peers)

    carry_copy().start()
    for i in range(half):
        pair_copy(i).start()
    for d in range(1, window + 1):

        @pl.when(me + d < span)
        def _():
            kv_copy(d, 0).start()
            kv_copy(d, 1).start()

        @pl.when(me < d)
        def _():
            keys[d * rows : (d + 1) * rows, :] = jnp.zeros((rows, width), bf16)
            values[d * rows : (d + 1) * rows, :] = jnp.zeros((rows, width), bf16)

    keys[0:rows, :] = soft_k[...]
    values[0:rows, :] = soft_v[...]

    mask = (s_at <= t_at) & (first + s_at >= doc_col)
    bias[:, 0:rows] = jnp.where(mask, 0.0, NEGATIVE)
    for d in range(1, window + 1):
        bias[:, d * rows : (d + 1) * rows] = jnp.where(
            first - d * rows + s_at >= doc_col, 0.0, NEGATIVE
        )
    for h in range(heads):
        query = head(lin_q, h)
        diff = cum[:, h : h + 1] - cum_rows[h : h + 1, :]
        decay = jnp.where(mask, jnp.exp(jnp.where(mask, diff, 0.0)), 0.0)
        scores = lax.dot_general(
            query, head(lin_k, h), (((1,), (1,)), ((), ())), preferred_element_type=f32
        )
        intra[h] = jnp.dot(
            (scores * decay).astype(bf16), head(lin_v, h), preferred_element_type=f32
        )
        queried[h] = (query.astype(f32) * entry[:, h : h + 1]).astype(bf16)

    carry_copy().wait_recv()
    even = x == 0
    for i in range(half):
        h = half * x + i
        pair_copy(i).wait_recv()
        own, far = local[h], paired[i].astype(f32)
        own_carry, far_carry = carries[pl.ds(h, 1), :], carries_in[pl.ds(h, 1), :]
        early, late = jnp.where(even, own, far), jnp.where(even, far, own)
        early_carry = jnp.where(even, own_carry, far_carry)
        late_carry = jnp.where(even, far_carry, own_carry)

        @pl.when(z == 0)
        def _():
            arrived[i] = jnp.zeros((width, width), bf16)

        @pl.when(z > 0)
        def _():
            chain_copy(i).wait_recv()

        entering_even = arrived[i].astype(f32)
        entering_odd = early + early_carry * entering_even
        onward[i] = (late + late_carry * entering_odd).astype(bf16)

        @pl.when(me + 2 < span)
        def _():
            chain_copy(i).start()

        incoming[h] = jnp.where(even, entering_even, entering_odd).astype(bf16)
        across[i] = jnp.where(even, entering_odd, entering_even).astype(bf16)
        state_copy(i).start()

    for d in range(1, window + 1):

        @pl.when(me >= d)
        def _():
            kv_copy(d, 0).wait_recv()
            kv_copy(d, 1).wait_recv()

    factor = math.log2(math.e) / math.sqrt(width)
    for h in range(heads):
        scores = lax.dot_general(
            head(soft_q, h), keys[...], (((1,), (1,)), ((), ())), preferred_element_type=f32
        )
        scores = scores + bias[...]
        peak = jnp.max(scores, axis=1, keepdims=True)
        weights = jnp.exp2((scores - peak) * factor)
        total = jnp.sum(weights, axis=1, keepdims=True)
        numer = jnp.dot(weights.astype(bf16), values[...], preferred_element_type=f32)
        soft_out[:, h * width : (h + 1) * width] = (numer / total).astype(bf16)

    for i in range(half):
        state_copy(i).wait_recv()
    for h in range(heads):
        summed = intra[h] + jnp.dot(queried[h], incoming[h], preferred_element_type=f32)
        mean_square = jnp.mean(summed * summed, axis=1, keepdims=True)
        normed = summed * lax.rsqrt(mean_square + 1e-06) * head(gain, h)
        lin_out[:, h * width : (h + 1) * width] = normed.astype(bf16)

    carry_copy().wait_send()
    for i in range(half):
        pair_copy(i).wait_send()
        state_copy(i).wait_send()

        @pl.when(me + 2 < span)
        def _():
            chain_copy(i).wait_send()

    for d in range(1, window + 1):

        @pl.when(me + d < span)
        def _():
            kv_copy(d, 0).wait_send()
            kv_copy(d, 1).wait_send()


def in_one_kernel(
    lin_query,
    lin_key,
    lin_value,
    forget_log,
    norm_gain,
    soft_query,
    soft_key,
    soft_value,
    doc_lengths,
):
    span = lax.axis_size("seq")
    rows, columns = lin_query.shape
    heads = columns // HEAD_DIM
    half, window = heads // 2, span // 2
    f32, bf16 = jnp.float32, jnp.bfloat16
    dma = pltpu.SemaphoreType.DMA
    whole = pl.BlockSpec(memory_space=pltpu.VMEM)
    square = (HEAD_DIM, HEAD_DIM)
    return pl.pallas_call(
        functools.partial(block_kernel, span, heads),
        out_shape=(
            jax.ShapeDtypeStruct((rows, columns), bf16),
            jax.ShapeDtypeStruct((rows, columns), bf16),
        ),
        in_specs=[pl.BlockSpec(memory_space=pltpu.SMEM)] + [whole] * 8,
        out_specs=(whole, whole),
        scratch_shapes=[
            pltpu.VMEM(((window + 1) * rows, HEAD_DIM), bf16),
            pltpu.VMEM(((window + 1) * rows, HEAD_DIM), bf16),
            pltpu.VMEM((rows, (window + 1) * rows), f32),
            pltpu.VMEM((heads, *square), f32),
            pltpu.VMEM((heads, *square), bf16),
            pltpu.VMEM((half, *square), bf16),
            pltpu.VMEM((heads, HEAD_DIM), f32),
            pltpu.VMEM((heads, HEAD_DIM), f32),
            pltpu.VMEM((half, *square), bf16),
            pltpu.VMEM((half, *square), bf16),
            pltpu.VMEM((half, *square), bf16),
            pltpu.VMEM((heads, *square), bf16),
            pltpu.VMEM((heads, rows, HEAD_DIM), f32),
            pltpu.VMEM((heads, rows, HEAD_DIM), bf16),
            dma((2 * window,)),
            dma((2 * window,)),
            dma((half,)),
            dma((half,)),
            dma,
            dma,
            dma((half,)),
            dma((half,)),
            dma((half,)),
            dma((half,)),
        ],
        compiler_params=pltpu.CompilerParams(
            collective_id=0, has_side_effects=True, vmem_limit_bytes=32 << 20
        ),
    )(
        doc_lengths,
        lin_query,
        lin_key,
        lin_value,
        forget_log,
        norm_gain.reshape(1, columns),
        soft_query,
        soft_key,
        soft_value,
    )


def solution(mesh):
    placed = (
        P(("rep", "seq"), "sub"),
        P(("rep", "seq"), "sub"),
        P(("rep", "seq"), "sub"),
        P(("rep", "seq"), "sub"),
        P("sub"),
        P(("rep", "seq"), "sub"),
        P(("rep", "seq"), "sub"),
        P(("rep", "seq"), "sub"),
        P("rep", None),
    )
    small = mesh.shape["seq"] == 8
    return jax.shard_map(
        in_one_kernel if small else per_device,
        mesh=mesh,
        in_specs=placed,
        out_specs=(P(("rep", "seq"), "sub"), P(("rep", "seq"), "sub")),
        check_vma=False,
    )
```

```python
import functools
import math

import jax
import jax.numpy as jnp
from jax import lax
from jax.experimental import pallas as pl
from jax.experimental.pallas import tpu as pltpu
from jax.sharding import PartitionSpec as P

HEAD_DIM = 128


NEGATIVE = -1e30


def entering(array, axis, combine, identity):
    size, mine = (lax.axis_size(axis), lax.axis_index(axis))
    everything = jax.tree.map(
        lambda part, kind: lax.all_gather(part.astype(kind), axis),
        array,
        (jnp.bfloat16, jnp.bfloat16),
    )
    start = jax.tree.map(
        lambda part, zero: jnp.broadcast_to(jnp.asarray(zero, part.dtype), part.shape),
        array,
        identity,
    )

    def step(k, before):
        reached = k < mine
        new = combine(
            before, jax.tree.map(lambda part, own: part[k].astype(own.dtype), everything, array)
        )
        return jax.tree.map(lambda a, b: jnp.where(reached, a, b), new, before)

    return lax.fori_loop(0, size, step, start)


def passed_along(block, axis, distance):
    devices = range(lax.axis_size(axis))
    route = [(i - distance, i) for i in devices if i - distance in devices]
    return lax.ppermute(block, axis, route)


def document_ids(lengths_row, where_at):
    starts = jnp.cumsum(lengths_row) - lengths_row
    ids = jnp.sum((starts[None, :] <= where_at[:, None]).astype(jnp.int32), axis=1) - 1
    begins = jnp.any(starts[None, :] == where_at[:, None], axis=1)
    return (ids, begins)


def linear_parts(lin_query, lin_key, lin_value, forget_log, ids, begins):
    rows_here, heads_here = forget_log.shape
    queries = lin_query.reshape(rows_here, heads_here, HEAD_DIM)
    keys = lin_key.reshape(rows_here, heads_here, HEAD_DIM)
    values = lin_value.reshape(rows_here, heads_here, HEAD_DIM)
    cum = jnp.cumsum(forget_log, axis=0)
    live = (jnp.cumsum(begins.astype(jnp.int32)) == 0).astype(jnp.float32)
    order = jnp.arange(rows_here, dtype=jnp.int32)
    mask = (ids[:, None] == ids[None, :]) & (order[None, :] <= order[:, None])
    diff = cum.T[:, :, None] - cum.T[:, None, :]
    decay = jnp.where(mask[None], jnp.exp(jnp.where(mask[None], diff, 0.0)), 0.0)
    scores = jnp.einsum("thd,shd->hts", queries, keys, preferred_element_type=jnp.float32)
    weights = (scores * decay).astype(jnp.bfloat16)
    intra = jnp.einsum("hts,shd->thd", weights, values, preferred_element_type=jnp.float32)
    tail_mask = ids == ids[-1]
    tail = jnp.where(
        tail_mask[:, None], jnp.exp(jnp.where(tail_mask[:, None], cum[-1][None, :] - cum, 0.0)), 0.0
    )
    keyed = (keys * tail[:, :, None]).astype(jnp.bfloat16)
    local_state = jnp.einsum("shd,she->hde", keyed, values, preferred_element_type=jnp.float32)
    block_decay = jnp.exp(cum[-1]) * live[-1]
    queried = (queries * (jnp.exp(cum) * live[:, None])[:, :, None]).astype(jnp.bfloat16)
    return (intra, queried, local_state, block_decay)


def linear_finish(intra, queried, incoming, norm_gain):
    rows_here, heads_here, width = intra.shape
    inter = jnp.einsum(
        "thd,hde->the", queried, incoming.astype(jnp.bfloat16), preferred_element_type=jnp.float32
    )
    summed = intra + inter
    mean_square = jnp.mean(summed * summed, axis=-1, keepdims=True)
    normed = summed * lax.rsqrt(mean_square + 1e-06) * norm_gain.reshape(heads_here, width)
    return normed.reshape(rows_here, heads_here * width).astype(jnp.bfloat16)


def attend(running, queries, key_block, value_block, mask):
    peak, total, accum = running
    width = queries.shape[-1]
    scores = jnp.einsum(
        "tkgd,skd->kgts", queries, key_block, preferred_element_type=jnp.float32
    ) * (1.0 / math.sqrt(width))
    scores = jnp.where(mask, scores, NEGATIVE)
    new_peak = jnp.maximum(peak, jnp.max(scores, axis=-1))
    weights = jnp.where(mask, jnp.exp(scores - new_peak[..., None]), 0.0)
    rescale = jnp.exp(peak - new_peak)
    total = total * rescale + jnp.sum(weights, axis=-1)
    accum = accum * rescale[..., None] + jnp.einsum(
        "kgts,skd->kgtd",
        weights.astype(jnp.bfloat16),
        value_block,
        preferred_element_type=jnp.float32,
    )
    return (new_peak, total, accum)


def start_running(kv_here, group, count):
    return (
        jnp.full((kv_here, group, count), NEGATIVE, jnp.float32),
        jnp.zeros((kv_here, group, count), jnp.float32),
        jnp.zeros((kv_here, group, count, HEAD_DIM), jnp.float32),
    )


def finish_running(running, count, heads_here):
    peak, total, accum = running
    soft = (accum / total[..., None]).astype(jnp.bfloat16)
    return soft.transpose(2, 0, 1, 3).reshape(count, heads_here * HEAD_DIM)


def per_device(
    lin_query,
    lin_key,
    lin_value,
    forget_log,
    norm_gain,
    soft_query,
    soft_key,
    soft_value,
    doc_lengths,
):
    rows_here = lin_query.shape[0]
    seq_count = doc_lengths.shape[0]
    span = lax.axis_size("seq") // seq_count
    position = lax.axis_index("seq")
    rank = position % span
    lengths_row = doc_lengths[0]
    order = jnp.arange(rows_here, dtype=jnp.int32)
    query_where = rank * rows_here + order
    ids, begins = document_ids(lengths_row, query_where)
    intra, queried, local_state, block_decay = linear_parts(
        lin_query, lin_key, lin_value, forget_log, ids, begins
    )

    def combine_states(earlier, later):
        return (earlier[0] * later[0], later[0][:, None, None] * earlier[1] + later[1])

    identity = (jnp.ones_like(block_decay), jnp.zeros_like(local_state))
    scanned = entering((block_decay, local_state), "seq", combine_states, identity)
    lin_out = linear_finish(intra, queried, scanned[1], norm_gain)
    kv_here = soft_key.shape[1] // HEAD_DIM
    heads_here = soft_query.shape[1] // HEAD_DIM
    group = heads_here // kv_here
    queries = soft_query.reshape(rows_here, kv_here, group, HEAD_DIM)

    def piece_mask(start, count):
        key_where = start + jnp.arange(count, dtype=jnp.int32)
        source_ids, unused = document_ids(lengths_row, key_where)
        return (ids[:, None] == source_ids[None, :]) & (key_where[None, :] <= query_where[:, None])

    def attend_piece(running, key_piece, value_piece, start):
        count = key_piece.shape[0]
        key_block = key_piece.reshape(count, kv_here, HEAD_DIM)
        value_block = value_piece.reshape(count, kv_here, HEAD_DIM)
        return attend(running, queries, key_block, value_block, piece_mask(start, count))

    own_pair = jnp.stack([soft_key, soft_value])
    running = attend_piece(
        start_running(kv_here, group, rows_here), soft_key, soft_value, rank * rows_here
    )

    def visit_cycle(turn, state):
        moving, inner_state = state
        moving = passed_along(moving, "seq", 1)
        source = rank - turn - 1
        inner_state = lax.cond(
            source >= 0,
            lambda inner: attend_piece(inner, moving[0], moving[1], source * rows_here),
            lambda inner: inner,
            inner_state,
        )
        return (moving, inner_state)

    unused_pair, running = lax.fori_loop(0, span - 1, visit_cycle, (own_pair, running))
    soft_out = finish_running(running, rows_here, heads_here)
    return (lin_out, soft_out)


def block_kernel(
    span,
    heads,
    lens,
    lin_q_far,
    lin_k_far,
    lin_v_far,
    forget_far,
    gain_far,
    soft_q_far,
    soft_k_far,
    soft_v_far,
    lin_out,
    soft_out,
    lin_q,
    lin_k,
    lin_v,
    forget,
    gain,
    soft_q,
    pairs,
    bias,
    local,
    packed,
    paired,
    carries,
    carries_in,
    arrived,
    onward,
    across,
    incoming,
    intra,
    queried,
    loads,
    send_kv,
    recv_kv,
    send_pair,
    recv_pair,
    send_carry,
    recv_carry,
    send_chain,
    recv_chain,
    send_state,
    recv_state,
):
    f32, bf16 = jnp.float32, jnp.bfloat16
    rows = lin_q.shape[0]
    width = HEAD_DIM
    half = heads // 2
    window = span // 2
    me = lax.axis_index("seq")
    z, x = me // 2, me % 2
    other = me + 1 - 2 * x
    mesh_id = pl.DeviceIdType.MESH

    def load(i):
        src, dst = (
            (soft_k_far, pairs.at[0, 0]),
            (soft_v_far, pairs.at[0, 1]),
            (forget_far, forget),
            (lin_k_far, lin_k),
            (lin_v_far, lin_v),
            (lin_q_far, lin_q),
            (soft_q_far, soft_q),
            (gain_far, gain),
        )[i]
        return pltpu.make_async_copy(src, dst, loads.at[i])

    barrier = pltpu.get_barrier_semaphore()
    near = [(other, True)]
    for d in (2, 4):
        near += [(me + d, me + d < span), (me - d, me >= d)]
    peers = 0
    for target, ok in near:
        peers = peers + jnp.int32(ok)

        @pl.when(ok)
        def _():
            pl.semaphore_signal(barrier, inc=1, device_id={"seq": target}, device_id_type=mesh_id)

    for i in range(8):
        load(i).start()

    def remote(src, dst, send, recv, target):
        return pltpu.make_async_remote_copy(
            src_ref=src,
            dst_ref=dst,
            send_sem=send,
            recv_sem=recv,
            device_id={"seq": target},
            device_id_type=mesh_id,
        )

    def kv_copy(held, slot, ahead):
        return remote(pairs.at[held], pairs.at[slot], send_kv.at[slot], recv_kv.at[slot], me + ahead)

    first_column, second_column = x == 0, x == 1
    kv_sent = (
        (0, 2, 2, me + 2 < span),
        (0, 4, 4, me + 4 < span),
        (0, 1, 1, first_column),
    )
    kv_passed = (
        (2, 3, 1, first_column & (me >= 2)),
        (2, 1, -1, second_column & (me >= 2)),
        (4, 3, -1, second_column & (me >= 4)),
    )

    def pair_copy(i):
        return remote(
            packed.at[half * (1 - x) + i], paired.at[i], send_pair.at[i], recv_pair.at[i], other
        )

    def carry_copy():
        return remote(carries, carries_in, send_carry, recv_carry, other)

    def chain_copy(i):
        return remote(onward.at[i], arrived.at[i], send_chain.at[i], recv_chain.at[i], me + 2)

    def state_copy(i):
        return remote(
            across.at[i], incoming.at[half * x + i], send_state.at[i], recv_state.at[i], other
        )

    load(0).wait()
    load(1).wait()
    pl.semaphore_wait(barrier, peers)
    for held, slot, ahead, ok in kv_sent:

        @pl.when(ok)
        def _():
            kv_copy(held, slot, ahead).start()

    first = me * rows
    starts = [jnp.int32(0)]
    for i in range(lens.shape[1] - 1):
        starts.append(starts[-1] + lens[0, i])
    where_col = first + lax.broadcasted_iota(jnp.int32, (rows, 1), 0)
    doc_col = jnp.zeros((rows, 1), jnp.int32)
    live_col = jnp.ones((rows, 1), f32)
    last = first + rows - 1
    doc_last = jnp.int32(0)
    live_last = jnp.float32(1.0)
    for s in starts:
        doc_col = jnp.maximum(doc_col, jnp.where(where_col >= s, s, 0))
        live_col = jnp.where((where_col >= s) & (s >= first), 0.0, live_col)
        doc_last = jnp.maximum(doc_last, jnp.where(last >= s, s, 0))
        live_last = jnp.where((last >= s) & (s >= first), 0.0, live_last)

    t_at = lax.broadcasted_iota(jnp.int32, (rows, rows), 0)
    s_at = lax.broadcasted_iota(jnp.int32, (rows, rows), 1)
    tri = (s_at <= t_at).astype(f32)
    load(2).wait()
    logs = forget[...]
    cum = lax.dot_general(
        tri, logs, (((1,), (1,)), ((), ())), precision=lax.Precision.HIGHEST,
        preferred_element_type=f32,
    )
    cum_rows = lax.dot_general(
        logs, tri, (((1,), (1,)), ((), ())), precision=lax.Precision.HIGHEST,
        preferred_element_type=f32,
    )
    end = cum[rows - 1 : rows, :]
    tail_mask = where_col >= doc_last
    tail = jnp.where(tail_mask, jnp.exp(jnp.where(tail_mask, end - cum, 0.0)), 0.0)
    entry = jnp.exp(cum) * live_col
    carries[...] = jnp.broadcast_to(jnp.exp(cum_rows[:, rows - 1 : rows]) * live_last, carries.shape)

    def head(ref, h):
        return ref[:, h * width : (h + 1) * width]

    load(3).wait()
    load(4).wait()
    for h in range(heads):
        keyed = (head(lin_k, h).astype(f32) * tail[:, h : h + 1]).astype(bf16)
        state = lax.dot_general(
            keyed, head(lin_v, h), (((0,), (0,)), ((), ())), preferred_element_type=f32
        )
        local[h] = state
        packed[h] = state.astype(bf16)

    carry_copy().start()
    for i in range(half):
        pair_copy(i).start()
    for d in range(1, window + 1):

        @pl.when(me < d)
        def _():
            pairs[d] = jnp.zeros((2, rows, width), bf16)

    mask = (s_at <= t_at) & (first + s_at >= doc_col)
    bias[:, 0:rows] = jnp.where(mask, 0.0, NEGATIVE)
    for d in range(1, window + 1):
        bias[:, d * rows : (d + 1) * rows] = jnp.where(
            first - d * rows + s_at >= doc_col, 0.0, NEGATIVE
        )
    load(5).wait()
    for h in range(heads):
        query = head(lin_q, h)
        diff = cum[:, h : h + 1] - cum_rows[h : h + 1, :]
        decay = jnp.where(mask, jnp.exp(jnp.where(mask, diff, 0.0)), 0.0)
        scores = lax.dot_general(
            query, head(lin_k, h), (((1,), (1,)), ((), ())), preferred_element_type=f32
        )
        intra[h] = jnp.dot(
            (scores * decay).astype(bf16), head(lin_v, h), preferred_element_type=f32
        )
        queried[h] = (query.astype(f32) * entry[:, h : h + 1]).astype(bf16)

    for d in (2, 4):

        @pl.when(me >= d)
        def _():
            kv_copy(0, d, d).wait_recv()

    for held, slot, ahead, ok in kv_passed:

        @pl.when(ok)
        def _():
            kv_copy(held, slot, ahead).start()

    load(6).wait()
    load(7).wait()

    def softmax():
        key_rows = pairs[:, 0].reshape((window + 1) * rows, width)
        value_rows = pairs[:, 1].reshape((window + 1) * rows, width)
        factor = math.log2(math.e) / math.sqrt(width)
        for h in range(heads):
            scores = lax.dot_general(
                head(soft_q, h), key_rows, (((1,), (1,)), ((), ())), preferred_element_type=f32
            )
            scores = scores + bias[...]
            peak = jnp.max(scores, axis=1, keepdims=True)
            weights = jnp.exp2((scores - peak) * factor)
            total = jnp.sum(weights, axis=1, keepdims=True)
            numer = jnp.dot(weights.astype(bf16), value_rows, preferred_element_type=f32)
            soft_out[:, h * width : (h + 1) * width] = (numer / total).astype(bf16)

    def odd_slots():
        for d in (1, 3):

            @pl.when(me >= d)
            def _():
                kv_copy(0, d, 1).wait_recv()

    z_last = span // 2 - 1

    @pl.when(z == z_last)
    def _():
        odd_slots()
        softmax()

    carry_copy().wait_recv()
    even = x == 0
    for i in range(half):
        h = half * x + i
        pair_copy(i).wait_recv()
        own, far = local[h], paired[i].astype(f32)
        own_carry, far_carry = carries[pl.ds(h, 1), :], carries_in[pl.ds(h, 1), :]
        early, late = jnp.where(even, own, far), jnp.where(even, far, own)
        early_carry = jnp.where(even, own_carry, far_carry)
        late_carry = jnp.where(even, far_carry, own_carry)

        @pl.when(z == 0)
        def _():
            arrived[i] = jnp.zeros((width, width), bf16)

        @pl.when(z > 0)
        def _():
            chain_copy(i).wait_recv()

        entering_even = arrived[i].astype(f32)
        entering_odd = early + early_carry * entering_even
        onward[i] = (late + late_carry * entering_odd).astype(bf16)

        @pl.when(me + 2 < span)
        def _():
            chain_copy(i).start()

        incoming[h] = jnp.where(even, entering_even, entering_odd).astype(bf16)
        across[i] = jnp.where(even, entering_odd, entering_even).astype(bf16)
        state_copy(i).start()

    @pl.when(z < z_last)
    def _():
        odd_slots()
        softmax()

    for i in range(half):
        state_copy(i).wait_recv()
    for h in range(heads):
        summed = intra[h] + jnp.dot(queried[h], incoming[h], preferred_element_type=f32)
        mean_square = jnp.mean(summed * summed, axis=1, keepdims=True)
        normed = summed * lax.rsqrt(mean_square + 1e-06) * head(gain, h)
        lin_out[:, h * width : (h + 1) * width] = normed.astype(bf16)

    carry_copy().wait_send()
    for i in range(half):
        pair_copy(i).wait_send()
        state_copy(i).wait_send()

        @pl.when(me + 2 < span)
        def _():
            chain_copy(i).wait_send()

    for held, slot, ahead, ok in kv_sent + kv_passed:

        @pl.when(ok)
        def _():
            kv_copy(held, slot, ahead).wait_send()


def in_one_kernel(
    lin_query,
    lin_key,
    lin_value,
    forget_log,
    norm_gain,
    soft_query,
    soft_key,
    soft_value,
    doc_lengths,
):
    span = lax.axis_size("seq")
    rows, columns = lin_query.shape
    heads = columns // HEAD_DIM
    half, window = heads // 2, span // 2
    f32, bf16 = jnp.float32, jnp.bfloat16
    dma = pltpu.SemaphoreType.DMA
    whole = pl.BlockSpec(memory_space=pltpu.VMEM)
    square = (HEAD_DIM, HEAD_DIM)
    return pl.pallas_call(
        functools.partial(block_kernel, span, heads),
        out_shape=(
            jax.ShapeDtypeStruct((rows, columns), bf16),
            jax.ShapeDtypeStruct((rows, columns), bf16),
        ),
        in_specs=[pl.BlockSpec(memory_space=pltpu.SMEM)]
        + [pl.BlockSpec(memory_space=pltpu.HBM)] * 8,
        out_specs=(whole, whole),
        scratch_shapes=[
            pltpu.VMEM((rows, columns), bf16),
            pltpu.VMEM((rows, columns), bf16),
            pltpu.VMEM((rows, columns), bf16),
            pltpu.VMEM((heads, rows), f32),
            pltpu.VMEM((1, columns), f32),
            pltpu.VMEM((rows, columns), bf16),
            pltpu.VMEM((window + 1, 2, rows, HEAD_DIM), bf16),
            pltpu.VMEM((rows, (window + 1) * rows), f32),
            pltpu.VMEM((heads, *square), f32),
            pltpu.VMEM((heads, *square), bf16),
            pltpu.VMEM((half, *square), bf16),
            pltpu.VMEM((heads, HEAD_DIM), f32),
            pltpu.VMEM((heads, HEAD_DIM), f32),
            pltpu.VMEM((half, *square), bf16),
            pltpu.VMEM((half, *square), bf16),
            pltpu.VMEM((half, *square), bf16),
            pltpu.VMEM((heads, *square), bf16),
            pltpu.VMEM((heads, rows, HEAD_DIM), f32),
            pltpu.VMEM((heads, rows, HEAD_DIM), bf16),
            dma((8,)),
            dma((window + 1,)),
            dma((window + 1,)),
            dma((half,)),
            dma((half,)),
            dma,
            dma,
            dma((half,)),
            dma((half,)),
            dma((half,)),
            dma((half,)),
        ],
        compiler_params=pltpu.CompilerParams(
            collective_id=0, has_side_effects=True, vmem_limit_bytes=62 << 20
        ),
    )(
        doc_lengths,
        lin_query,
        lin_key,
        lin_value,
        forget_log.T,
        norm_gain.reshape(1, columns),
        soft_query,
        soft_key,
        soft_value,
    )


def solution(mesh):
    placed = (
        P(("rep", "seq"), "sub"),
        P(("rep", "seq"), "sub"),
        P(("rep", "seq"), "sub"),
        P(("rep", "seq"), "sub"),
        P("sub"),
        P(("rep", "seq"), "sub"),
        P(("rep", "seq"), "sub"),
        P(("rep", "seq"), "sub"),
        P("rep", None),
    )
    small = mesh.shape["seq"] == 8
    return jax.shard_map(
        in_one_kernel if small else per_device,
        mesh=mesh,
        in_specs=placed,
        out_specs=(P(("rep", "seq"), "sub"), P(("rep", "seq"), "sub")),
        check_vma=False,
    )
```

```python
import functools
import math

import jax
import jax.numpy as jnp
from jax import lax
from jax.experimental import pallas as pl
from jax.experimental.pallas import tpu as pltpu
from jax.sharding import PartitionSpec as P

HEAD_DIM = 128


NEGATIVE = -1e30


def entering(array, axis, combine, identity):
    size, mine = (lax.axis_size(axis), lax.axis_index(axis))
    everything = jax.tree.map(
        lambda part, kind: lax.all_gather(part.astype(kind), axis),
        array,
        (jnp.bfloat16, jnp.bfloat16),
    )
    start = jax.tree.map(
        lambda part, zero: jnp.broadcast_to(jnp.asarray(zero, part.dtype), part.shape),
        array,
        identity,
    )

    def step(k, before):
        reached = k < mine
        new = combine(
            before, jax.tree.map(lambda part, own: part[k].astype(own.dtype), everything, array)
        )
        return jax.tree.map(lambda a, b: jnp.where(reached, a, b), new, before)

    return lax.fori_loop(0, size, step, start)


def passed_along(block, axis, distance):
    devices = range(lax.axis_size(axis))
    route = [(i - distance, i) for i in devices if i - distance in devices]
    return lax.ppermute(block, axis, route)


def document_ids(lengths_row, where_at):
    starts = jnp.cumsum(lengths_row) - lengths_row
    ids = jnp.sum((starts[None, :] <= where_at[:, None]).astype(jnp.int32), axis=1) - 1
    begins = jnp.any(starts[None, :] == where_at[:, None], axis=1)
    return (ids, begins)


def linear_parts(lin_query, lin_key, lin_value, forget_log, ids, begins):
    rows_here, heads_here = forget_log.shape
    queries = lin_query.reshape(rows_here, heads_here, HEAD_DIM)
    keys = lin_key.reshape(rows_here, heads_here, HEAD_DIM)
    values = lin_value.reshape(rows_here, heads_here, HEAD_DIM)
    cum = jnp.cumsum(forget_log, axis=0)
    live = (jnp.cumsum(begins.astype(jnp.int32)) == 0).astype(jnp.float32)
    order = jnp.arange(rows_here, dtype=jnp.int32)
    mask = (ids[:, None] == ids[None, :]) & (order[None, :] <= order[:, None])
    diff = cum.T[:, :, None] - cum.T[:, None, :]
    decay = jnp.where(mask[None], jnp.exp(jnp.where(mask[None], diff, 0.0)), 0.0)
    scores = jnp.einsum("thd,shd->hts", queries, keys, preferred_element_type=jnp.float32)
    weights = (scores * decay).astype(jnp.bfloat16)
    intra = jnp.einsum("hts,shd->thd", weights, values, preferred_element_type=jnp.float32)
    tail_mask = ids == ids[-1]
    tail = jnp.where(
        tail_mask[:, None], jnp.exp(jnp.where(tail_mask[:, None], cum[-1][None, :] - cum, 0.0)), 0.0
    )
    keyed = (keys * tail[:, :, None]).astype(jnp.bfloat16)
    local_state = jnp.einsum("shd,she->hde", keyed, values, preferred_element_type=jnp.float32)
    block_decay = jnp.exp(cum[-1]) * live[-1]
    queried = (queries * (jnp.exp(cum) * live[:, None])[:, :, None]).astype(jnp.bfloat16)
    return (intra, queried, local_state, block_decay)


def linear_finish(intra, queried, incoming, norm_gain):
    rows_here, heads_here, width = intra.shape
    inter = jnp.einsum(
        "thd,hde->the", queried, incoming.astype(jnp.bfloat16), preferred_element_type=jnp.float32
    )
    summed = intra + inter
    mean_square = jnp.mean(summed * summed, axis=-1, keepdims=True)
    normed = summed * lax.rsqrt(mean_square + 1e-06) * norm_gain.reshape(heads_here, width)
    return normed.reshape(rows_here, heads_here * width).astype(jnp.bfloat16)


def attend(running, queries, key_block, value_block, mask):
    peak, total, accum = running
    width = queries.shape[-1]
    scores = jnp.einsum(
        "tkgd,skd->kgts", queries, key_block, preferred_element_type=jnp.float32
    ) * (1.0 / math.sqrt(width))
    scores = jnp.where(mask, scores, NEGATIVE)
    new_peak = jnp.maximum(peak, jnp.max(scores, axis=-1))
    weights = jnp.where(mask, jnp.exp(scores - new_peak[..., None]), 0.0)
    rescale = jnp.exp(peak - new_peak)
    total = total * rescale + jnp.sum(weights, axis=-1)
    accum = accum * rescale[..., None] + jnp.einsum(
        "kgts,skd->kgtd",
        weights.astype(jnp.bfloat16),
        value_block,
        preferred_element_type=jnp.float32,
    )
    return (new_peak, total, accum)


def start_running(kv_here, group, count):
    return (
        jnp.full((kv_here, group, count), NEGATIVE, jnp.float32),
        jnp.zeros((kv_here, group, count), jnp.float32),
        jnp.zeros((kv_here, group, count, HEAD_DIM), jnp.float32),
    )


def finish_running(running, count, heads_here):
    peak, total, accum = running
    soft = (accum / total[..., None]).astype(jnp.bfloat16)
    return soft.transpose(2, 0, 1, 3).reshape(count, heads_here * HEAD_DIM)


def per_device(
    lin_query,
    lin_key,
    lin_value,
    forget_log,
    norm_gain,
    soft_query,
    soft_key,
    soft_value,
    doc_lengths,
):
    rows_here = lin_query.shape[0]
    seq_count = doc_lengths.shape[0]
    span = lax.axis_size("seq") // seq_count
    position = lax.axis_index("seq")
    rank = position % span
    lengths_row = doc_lengths[0]
    order = jnp.arange(rows_here, dtype=jnp.int32)
    query_where = rank * rows_here + order
    ids, begins = document_ids(lengths_row, query_where)
    intra, queried, local_state, block_decay = linear_parts(
        lin_query, lin_key, lin_value, forget_log, ids, begins
    )

    def combine_states(earlier, later):
        return (earlier[0] * later[0], later[0][:, None, None] * earlier[1] + later[1])

    identity = (jnp.ones_like(block_decay), jnp.zeros_like(local_state))
    scanned = entering((block_decay, local_state), "seq", combine_states, identity)
    lin_out = linear_finish(intra, queried, scanned[1], norm_gain)
    kv_here = soft_key.shape[1] // HEAD_DIM
    heads_here = soft_query.shape[1] // HEAD_DIM
    group = heads_here // kv_here
    queries = soft_query.reshape(rows_here, kv_here, group, HEAD_DIM)

    def piece_mask(start, count):
        key_where = start + jnp.arange(count, dtype=jnp.int32)
        source_ids, unused = document_ids(lengths_row, key_where)
        return (ids[:, None] == source_ids[None, :]) & (key_where[None, :] <= query_where[:, None])

    def attend_piece(running, key_piece, value_piece, start):
        count = key_piece.shape[0]
        key_block = key_piece.reshape(count, kv_here, HEAD_DIM)
        value_block = value_piece.reshape(count, kv_here, HEAD_DIM)
        return attend(running, queries, key_block, value_block, piece_mask(start, count))

    own_pair = jnp.stack([soft_key, soft_value])
    running = attend_piece(
        start_running(kv_here, group, rows_here), soft_key, soft_value, rank * rows_here
    )

    def visit_cycle(turn, state):
        moving, inner_state = state
        moving = passed_along(moving, "seq", 1)
        source = rank - turn - 1
        inner_state = lax.cond(
            source >= 0,
            lambda inner: attend_piece(inner, moving[0], moving[1], source * rows_here),
            lambda inner: inner,
            inner_state,
        )
        return (moving, inner_state)

    unused_pair, running = lax.fori_loop(0, span - 1, visit_cycle, (own_pair, running))
    soft_out = finish_running(running, rows_here, heads_here)
    return (lin_out, soft_out)


def block_kernel(
    span,
    heads,
    lens,
    lin_q_far,
    lin_k_far,
    lin_v_far,
    forget_far,
    gain_far,
    soft_q_far,
    soft_k_far,
    soft_v_far,
    lin_out,
    soft_out,
    lin_q,
    lin_k,
    lin_v,
    forget,
    gain,
    soft_q,
    pairs,
    bias,
    local,
    packed,
    paired,
    carries,
    carries_in,
    arrived,
    onward,
    early_in,
    ahead_of,
    across,
    incoming,
    intra,
    queried,
    lin_part,
    soft_part,
    loads,
    stores,
    send_kv,
    recv_kv,
    send_pair,
    recv_pair,
    send_carry,
    recv_carry,
    send_chain,
    recv_chain,
    send_early,
    recv_early,
    send_state,
    recv_state,
):
    f32, bf16 = jnp.float32, jnp.bfloat16
    rows = lin_q.shape[0]
    width = HEAD_DIM
    half = heads // 2
    window = span // 2
    me = lax.axis_index("seq")
    z, x = me // 2, me % 2
    other = me + 1 - 2 * x
    mesh_id = pl.DeviceIdType.MESH

    def load(i):
        src, dst = (
            (soft_k_far, pairs.at[0, 0]),
            (soft_v_far, pairs.at[0, 1]),
            (forget_far, forget),
            (lin_k_far, lin_k),
            (lin_v_far, lin_v),
            (lin_q_far, lin_q),
            (soft_q_far, soft_q),
            (gain_far, gain),
        )[i]
        return pltpu.make_async_copy(src, dst, loads.at[i])

    barrier = pltpu.get_barrier_semaphore()
    near = [(other, True)]
    for d in (2, 4):
        near += [(me + d, me + d < span), (me - d, me >= d)]
    peers = 0
    for target, ok in near:
        peers = peers + jnp.int32(ok)

        @pl.when(ok)
        def _():
            pl.semaphore_signal(barrier, inc=1, device_id={"seq": target}, device_id_type=mesh_id)

    for i in range(8):
        load(i).start()

    def remote(src, dst, send, recv, target):
        return pltpu.make_async_remote_copy(
            src_ref=src,
            dst_ref=dst,
            send_sem=send,
            recv_sem=recv,
            device_id={"seq": target},
            device_id_type=mesh_id,
        )

    def kv_copy(held, slot, ahead):
        return remote(pairs.at[held], pairs.at[slot], send_kv.at[slot], recv_kv.at[slot], me + ahead)

    first_column, second_column = x == 0, x == 1
    kv_sent = (
        (0, 2, 2, me + 2 < span),
        (0, 4, 4, me + 4 < span),
    )
    kv_beside = ((0, 1, 1, first_column),)
    kv_passed = (
        (2, 3, 1, first_column & (me >= 2)),
        (2, 1, -1, second_column & (me >= 2)),
        (4, 3, -1, second_column & (me >= 4)),
    )

    def pair_copy(i):
        return remote(
            packed.at[i], paired.at[i], send_pair.at[i], recv_pair.at[i], other
        )

    def carry_copy():
        return remote(carries, carries_in, send_carry, recv_carry, other)

    def chain_copy(i):
        return remote(onward.at[i], arrived.at[i], send_chain.at[i], recv_chain.at[i], me + 2)

    def early_copy(i):
        return remote(ahead_of.at[i], early_in.at[i], send_early.at[i], recv_early.at[i], me + 2)

    def state_copy(i):
        return remote(
            across.at[i], incoming.at[half * x + i], send_state.at[i], recv_state.at[i], other
        )

    load(0).wait()
    load(1).wait()
    pl.semaphore_wait(barrier, peers)
    for held, slot, ahead, ok in kv_sent:

        @pl.when(ok)
        def _():
            kv_copy(held, slot, ahead).start()

    first = me * rows
    starts = [jnp.int32(0)]
    for i in range(lens.shape[1] - 1):
        starts.append(starts[-1] + lens[0, i])
    where_col = first + lax.broadcasted_iota(jnp.int32, (rows, 1), 0)
    doc_col = jnp.zeros((rows, 1), jnp.int32)
    live_col = jnp.ones((rows, 1), f32)
    last = first + rows - 1
    doc_last = jnp.int32(0)
    live_last = jnp.float32(1.0)
    for s in starts:
        doc_col = jnp.maximum(doc_col, jnp.where(where_col >= s, s, 0))
        live_col = jnp.where((where_col >= s) & (s >= first), 0.0, live_col)
        doc_last = jnp.maximum(doc_last, jnp.where(last >= s, s, 0))
        live_last = jnp.where((last >= s) & (s >= first), 0.0, live_last)

    t_at = lax.broadcasted_iota(jnp.int32, (rows, rows), 0)
    s_at = lax.broadcasted_iota(jnp.int32, (rows, rows), 1)
    tri = (s_at <= t_at).astype(f32)
    load(2).wait()
    logs = forget[...]
    cum = lax.dot_general(
        tri, logs, (((1,), (1,)), ((), ())), precision=lax.Precision.HIGHEST,
        preferred_element_type=f32,
    )
    cum_rows = lax.dot_general(
        logs, tri, (((1,), (1,)), ((), ())), precision=lax.Precision.HIGHEST,
        preferred_element_type=f32,
    )
    end = cum[rows - 1 : rows, :]
    tail_mask = where_col >= doc_last
    tail = jnp.where(tail_mask, jnp.exp(jnp.where(tail_mask, end - cum, 0.0)), 0.0)
    entry = jnp.exp(cum) * live_col
    carries[...] = jnp.broadcast_to(jnp.exp(cum_rows[:, rows - 1 : rows]) * live_last, carries.shape)

    def head(ref, h):
        return ref[:, h * width : (h + 1) * width]

    even = x == 0

    def lanes(h):
        return pl.ds(pl.multiple_of(h * width, width), width)

    carry_copy().start()
    load(3).wait()
    load(4).wait()
    for mine in (False, True):
        for i in range(half):
            h = half * x + i if mine else half * (1 - x) + i
            low, high = tail[:, i : i + 1], tail[:, half + i : half + i + 1]
            scale = jnp.where(even, low, high) if mine else jnp.where(even, high, low)
            keyed = (lin_k[:, lanes(h)].astype(f32) * scale).astype(bf16)
            state = lax.dot_general(
                keyed, lin_v[:, lanes(h)], (((0,), (0,)), ((), ())), preferred_element_type=f32
            )
            if mine:
                local[i] = state
            else:
                packed[i] = state.astype(bf16)
                pair_copy(i).start()
    for held, slot, ahead, ok in kv_beside:

        @pl.when(ok)
        def _():
            kv_copy(held, slot, ahead).start()

    for d in range(1, window + 1):

        @pl.when(me < d)
        def _():
            pairs[d] = jnp.zeros((2, rows, width), bf16)

    mask = (s_at <= t_at) & (first + s_at >= doc_col)
    bias[:, 0:rows] = jnp.where(mask, 0.0, NEGATIVE)
    for d in range(1, window + 1):
        bias[:, d * rows : (d + 1) * rows] = jnp.where(
            first - d * rows + s_at >= doc_col, 0.0, NEGATIVE
        )
    load(5).wait()
    for h in range(heads):
        query = head(lin_q, h)
        diff = cum[:, h : h + 1] - cum_rows[h : h + 1, :]
        decay = jnp.where(mask, jnp.exp(jnp.where(mask, diff, 0.0)), 0.0)
        scores = lax.dot_general(
            query, head(lin_k, h), (((1,), (1,)), ((), ())), preferred_element_type=f32
        )
        intra[h] = jnp.dot(
            (scores * decay).astype(bf16), head(lin_v, h), preferred_element_type=f32
        )
        queried[h] = (query.astype(f32) * entry[:, h : h + 1]).astype(bf16)

    def pass_on(slot_in):
        @pl.when(me >= slot_in)
        def _():
            kv_copy(0, slot_in, slot_in).wait_recv()

        for held, slot, ahead, ok in kv_passed:
            if held == slot_in:

                @pl.when(ok)
                def _():
                    kv_copy(held, slot, ahead).start()

    pass_on(2)
    load(6).wait()
    load(7).wait()

    def softmax():
        key_rows = pairs[:, 0].reshape((window + 1) * rows, width)
        value_rows = pairs[:, 1].reshape((window + 1) * rows, width)
        factor = math.log2(math.e) / math.sqrt(width)
        for h in range(heads):
            scores = lax.dot_general(
                head(soft_q, h), key_rows, (((1,), (1,)), ((), ())), preferred_element_type=f32
            )
            scores = scores + bias[...]
            peak = jnp.max(scores, axis=1, keepdims=True)
            weights = jnp.exp2((scores - peak) * factor)
            total = jnp.sum(weights, axis=1, keepdims=True)
            numer = jnp.dot(weights.astype(bf16), value_rows, preferred_element_type=f32)
            soft_part[:, h * width : (h + 1) * width] = (numer / total).astype(bf16)

    def odd_slots():
        for d in (1, 3):

            @pl.when(me >= d)
            def _():
                kv_copy(0, d, 1).wait_recv()

    carry_copy().wait_recv()

    def parts(i):
        h = half * x + i
        own, far = local[i], paired[i].astype(f32)
        own_carry, far_carry = carries[pl.ds(h, 1), :], carries_in[pl.ds(h, 1), :]
        early, late = jnp.where(even, own, far), jnp.where(even, far, own)
        early_carry = jnp.where(even, own_carry, far_carry)
        late_carry = jnp.where(even, far_carry, own_carry)
        return early, early_carry, late, late_carry

    for i in range(half):
        pair_copy(i).wait_recv()
        early, early_carry, late, late_carry = parts(i)
        pair = late + late_carry * early

        @pl.when(z == 0)
        def _():
            onward[i] = pair.astype(bf16)
            chain_copy(i).start()
            arrived[i] = jnp.zeros((width, width), bf16)

        @pl.when(z == 1)
        def _():
            ahead_of[i] = pair.astype(bf16)
            early_copy(i).start()

        @pl.when(z == 2)
        def _():
            early_copy(i).wait_recv()
            before = early_in[i].astype(f32)
            onward[i] = (pair + (late_carry * early_carry) * before).astype(bf16)
            chain_copy(i).start()

    pass_on(4)
    for i in range(half):
        early, early_carry, late, late_carry = parts(i)

        @pl.when(z > 0)
        def _():
            chain_copy(i).wait_recv()

        entering_even = arrived[i].astype(f32)
        entering_odd = early + early_carry * entering_even

        @pl.when(z == 1)
        def _():
            onward[i] = (late + late_carry * entering_odd).astype(bf16)
            chain_copy(i).start()

        across[i] = jnp.where(even, entering_odd, entering_even).astype(bf16)
        state_copy(i).start()
        incoming[half * x + i] = jnp.where(even, entering_even, entering_odd).astype(bf16)

    odd_slots()
    softmax()
    soft_store = pltpu.make_async_copy(soft_part, soft_out, stores.at[heads])
    soft_store.start()

    def lin_store(h):
        columns = pl.ds(h * width, width)
        return pltpu.make_async_copy(
            lin_part.at[:, columns], lin_out.at[:, columns], stores.at[h]
        )

    for i in range(half):
        state_copy(i).wait_recv()
    for h in range(heads):
        summed = intra[h] + jnp.dot(queried[h], incoming[h], preferred_element_type=f32)
        mean_square = jnp.mean(summed * summed, axis=1, keepdims=True)
        normed = summed * lax.rsqrt(mean_square + 1e-06) * head(gain, h)
        lin_part[:, h * width : (h + 1) * width] = normed.astype(bf16)
        lin_store(h).start()

    carry_copy().wait_send()
    for i in range(half):
        pair_copy(i).wait_send()
        state_copy(i).wait_send()

        @pl.when(me + 2 < span)
        def _():
            chain_copy(i).wait_send()

        @pl.when(z == 1)
        def _():
            early_copy(i).wait_send()

    for held, slot, ahead, ok in kv_sent + kv_beside + kv_passed:

        @pl.when(ok)
        def _():
            kv_copy(held, slot, ahead).wait_send()

    soft_store.wait()
    for h in range(heads):
        lin_store(h).wait()


def results_kernel(lin_in, soft_in, lin_out, soft_out, sems):
    copies = [
        pltpu.make_async_copy(lin_in, lin_out, sems.at[0]),
        pltpu.make_async_copy(soft_in, soft_out, sems.at[1]),
    ]
    for copy in copies:
        copy.start()
    for copy in copies:
        copy.wait()


def in_one_kernel(
    lin_query,
    lin_key,
    lin_value,
    forget_log,
    norm_gain,
    soft_query,
    soft_key,
    soft_value,
    doc_lengths,
):
    span = lax.axis_size("seq")
    rows, columns = lin_query.shape
    heads = columns // HEAD_DIM
    half, window = heads // 2, span // 2
    f32, bf16 = jnp.float32, jnp.bfloat16
    dma = pltpu.SemaphoreType.DMA
    far = pl.BlockSpec(memory_space=pltpu.HBM)
    square = (HEAD_DIM, HEAD_DIM)
    shapes = (jax.ShapeDtypeStruct((rows, columns), bf16),) * 2
    lin_out, soft_out = pl.pallas_call(
        functools.partial(block_kernel, span, heads),
        out_shape=shapes,
        in_specs=[pl.BlockSpec(memory_space=pltpu.SMEM)]
        + [far] * 8,
        out_specs=(far, far),
        scratch_shapes=[
            pltpu.VMEM((rows, columns), bf16),
            pltpu.VMEM((rows, columns), bf16),
            pltpu.VMEM((rows, columns), bf16),
            pltpu.VMEM((heads, rows), f32),
            pltpu.VMEM((1, columns), f32),
            pltpu.VMEM((rows, columns), bf16),
            pltpu.VMEM((window + 1, 2, rows, HEAD_DIM), bf16),
            pltpu.VMEM((rows, (window + 1) * rows), f32),
            pltpu.VMEM((half, *square), f32),
            pltpu.VMEM((half, *square), bf16),
            pltpu.VMEM((half, *square), bf16),
            pltpu.VMEM((heads, HEAD_DIM), f32),
            pltpu.VMEM((heads, HEAD_DIM), f32),
            pltpu.VMEM((half, *square), bf16),
            pltpu.VMEM((half, *square), bf16),
            pltpu.VMEM((half, *square), bf16),
            pltpu.VMEM((half, *square), bf16),
            pltpu.VMEM((half, *square), bf16),
            pltpu.VMEM((heads, *square), bf16),
            pltpu.VMEM((heads, rows, HEAD_DIM), f32),
            pltpu.VMEM((heads, rows, HEAD_DIM), bf16),
            pltpu.VMEM((rows, columns), bf16),
            pltpu.VMEM((rows, columns), bf16),
            dma((8,)),
            dma((heads + 1,)),
            dma((window + 1,)),
            dma((window + 1,)),
            dma((half,)),
            dma((half,)),
            dma,
            dma,
            dma((half,)),
            dma((half,)),
            dma((half,)),
            dma((half,)),
            dma((half,)),
            dma((half,)),
        ],
        compiler_params=pltpu.CompilerParams(
            collective_id=0, has_side_effects=True, vmem_limit_bytes=62 << 20
        ),
    )(
        doc_lengths,
        lin_query,
        lin_key,
        lin_value,
        forget_log.T,
        norm_gain.reshape(1, columns),
        soft_query,
        soft_key,
        soft_value,
    )
    return pl.pallas_call(
        results_kernel,
        out_shape=shapes,
        in_specs=[far, far],
        out_specs=(far, far),
        scratch_shapes=[dma((2,))],
        compiler_params=pltpu.CompilerParams(vmem_limit_bytes=62 << 20),
    )(lin_out, soft_out)


def solution(mesh):
    placed = (
        P(("rep", "seq"), "sub"),
        P(("rep", "seq"), "sub"),
        P(("rep", "seq"), "sub"),
        P(("rep", "seq"), "sub"),
        P("sub"),
        P(("rep", "seq"), "sub"),
        P(("rep", "seq"), "sub"),
        P(("rep", "seq"), "sub"),
        P("rep", None),
    )
    small = mesh.shape["seq"] == 8
    return jax.shard_map(
        in_one_kernel if small else per_device,
        mesh=mesh,
        in_specs=placed,
        out_specs=(P(("rep", "seq"), "sub"), P(("rep", "seq"), "sub")),
        check_vma=False,
    )
```

```python
import functools
import math

import jax
import jax.numpy as jnp
from jax import lax
from jax.experimental import pallas as pl
from jax.experimental.pallas import tpu as pltpu
from jax.sharding import PartitionSpec as P

HEAD_DIM = 128


NEGATIVE = -1e30


def entering(array, axis, combine, identity):
    size, mine = (lax.axis_size(axis), lax.axis_index(axis))
    everything = jax.tree.map(
        lambda part, kind: lax.all_gather(part.astype(kind), axis),
        array,
        (jnp.bfloat16, jnp.bfloat16),
    )
    start = jax.tree.map(
        lambda part, zero: jnp.broadcast_to(jnp.asarray(zero, part.dtype), part.shape),
        array,
        identity,
    )

    def step(k, before):
        reached = k < mine
        new = combine(
            before, jax.tree.map(lambda part, own: part[k].astype(own.dtype), everything, array)
        )
        return jax.tree.map(lambda a, b: jnp.where(reached, a, b), new, before)

    return lax.fori_loop(0, size, step, start)


def passed_along(block, axis, distance):
    devices = range(lax.axis_size(axis))
    route = [(i - distance, i) for i in devices if i - distance in devices]
    return lax.ppermute(block, axis, route)


def document_ids(lengths_row, where_at):
    starts = jnp.cumsum(lengths_row) - lengths_row
    ids = jnp.sum((starts[None, :] <= where_at[:, None]).astype(jnp.int32), axis=1) - 1
    begins = jnp.any(starts[None, :] == where_at[:, None], axis=1)
    return (ids, begins)


def linear_parts(lin_query, lin_key, lin_value, forget_log, ids, begins):
    rows_here, heads_here = forget_log.shape
    queries = lin_query.reshape(rows_here, heads_here, HEAD_DIM)
    keys = lin_key.reshape(rows_here, heads_here, HEAD_DIM)
    values = lin_value.reshape(rows_here, heads_here, HEAD_DIM)
    cum = jnp.cumsum(forget_log, axis=0)
    live = (jnp.cumsum(begins.astype(jnp.int32)) == 0).astype(jnp.float32)
    order = jnp.arange(rows_here, dtype=jnp.int32)
    mask = (ids[:, None] == ids[None, :]) & (order[None, :] <= order[:, None])
    diff = cum.T[:, :, None] - cum.T[:, None, :]
    decay = jnp.where(mask[None], jnp.exp(jnp.where(mask[None], diff, 0.0)), 0.0)
    scores = jnp.einsum("thd,shd->hts", queries, keys, preferred_element_type=jnp.float32)
    weights = (scores * decay).astype(jnp.bfloat16)
    intra = jnp.einsum("hts,shd->thd", weights, values, preferred_element_type=jnp.float32)
    tail_mask = ids == ids[-1]
    tail = jnp.where(
        tail_mask[:, None], jnp.exp(jnp.where(tail_mask[:, None], cum[-1][None, :] - cum, 0.0)), 0.0
    )
    keyed = (keys * tail[:, :, None]).astype(jnp.bfloat16)
    local_state = jnp.einsum("shd,she->hde", keyed, values, preferred_element_type=jnp.float32)
    block_decay = jnp.exp(cum[-1]) * live[-1]
    queried = (queries * (jnp.exp(cum) * live[:, None])[:, :, None]).astype(jnp.bfloat16)
    return (intra, queried, local_state, block_decay)


def linear_finish(intra, queried, incoming, norm_gain):
    rows_here, heads_here, width = intra.shape
    inter = jnp.einsum(
        "thd,hde->the", queried, incoming.astype(jnp.bfloat16), preferred_element_type=jnp.float32
    )
    summed = intra + inter
    mean_square = jnp.mean(summed * summed, axis=-1, keepdims=True)
    normed = summed * lax.rsqrt(mean_square + 1e-06) * norm_gain.reshape(heads_here, width)
    return normed.reshape(rows_here, heads_here * width).astype(jnp.bfloat16)


def attend(running, queries, key_block, value_block, mask):
    peak, total, accum = running
    width = queries.shape[-1]
    scores = jnp.einsum(
        "tkgd,skd->kgts", queries, key_block, preferred_element_type=jnp.float32
    ) * (1.0 / math.sqrt(width))
    scores = jnp.where(mask, scores, NEGATIVE)
    new_peak = jnp.maximum(peak, jnp.max(scores, axis=-1))
    weights = jnp.where(mask, jnp.exp(scores - new_peak[..., None]), 0.0)
    rescale = jnp.exp(peak - new_peak)
    total = total * rescale + jnp.sum(weights, axis=-1)
    accum = accum * rescale[..., None] + jnp.einsum(
        "kgts,skd->kgtd",
        weights.astype(jnp.bfloat16),
        value_block,
        preferred_element_type=jnp.float32,
    )
    return (new_peak, total, accum)


def start_running(kv_here, group, count):
    return (
        jnp.full((kv_here, group, count), NEGATIVE, jnp.float32),
        jnp.zeros((kv_here, group, count), jnp.float32),
        jnp.zeros((kv_here, group, count, HEAD_DIM), jnp.float32),
    )


def finish_running(running, count, heads_here):
    peak, total, accum = running
    soft = (accum / total[..., None]).astype(jnp.bfloat16)
    return soft.transpose(2, 0, 1, 3).reshape(count, heads_here * HEAD_DIM)


def per_device(
    lin_query,
    lin_key,
    lin_value,
    forget_log,
    norm_gain,
    soft_query,
    soft_key,
    soft_value,
    doc_lengths,
):
    rows_here = lin_query.shape[0]
    seq_count = doc_lengths.shape[0]
    span = lax.axis_size("seq") // seq_count
    position = lax.axis_index("seq")
    rank = position % span
    lengths_row = doc_lengths[0]
    order = jnp.arange(rows_here, dtype=jnp.int32)
    query_where = rank * rows_here + order
    ids, begins = document_ids(lengths_row, query_where)
    intra, queried, local_state, block_decay = linear_parts(
        lin_query, lin_key, lin_value, forget_log, ids, begins
    )

    def combine_states(earlier, later):
        return (earlier[0] * later[0], later[0][:, None, None] * earlier[1] + later[1])

    identity = (jnp.ones_like(block_decay), jnp.zeros_like(local_state))
    scanned = entering((block_decay, local_state), "seq", combine_states, identity)
    lin_out = linear_finish(intra, queried, scanned[1], norm_gain)
    kv_here = soft_key.shape[1] // HEAD_DIM
    heads_here = soft_query.shape[1] // HEAD_DIM
    group = heads_here // kv_here
    queries = soft_query.reshape(rows_here, kv_here, group, HEAD_DIM)

    def piece_mask(start, count):
        key_where = start + jnp.arange(count, dtype=jnp.int32)
        source_ids, unused = document_ids(lengths_row, key_where)
        return (ids[:, None] == source_ids[None, :]) & (key_where[None, :] <= query_where[:, None])

    def attend_piece(running, key_piece, value_piece, start):
        count = key_piece.shape[0]
        key_block = key_piece.reshape(count, kv_here, HEAD_DIM)
        value_block = value_piece.reshape(count, kv_here, HEAD_DIM)
        return attend(running, queries, key_block, value_block, piece_mask(start, count))

    own_pair = jnp.stack([soft_key, soft_value])
    running = attend_piece(
        start_running(kv_here, group, rows_here), soft_key, soft_value, rank * rows_here
    )

    def visit_cycle(turn, state):
        moving, inner_state = state
        moving = passed_along(moving, "seq", 1)
        source = rank - turn - 1
        inner_state = lax.cond(
            source >= 0,
            lambda inner: attend_piece(inner, moving[0], moving[1], source * rows_here),
            lambda inner: inner,
            inner_state,
        )
        return (moving, inner_state)

    unused_pair, running = lax.fori_loop(0, span - 1, visit_cycle, (own_pair, running))
    soft_out = finish_running(running, rows_here, heads_here)
    return (lin_out, soft_out)


def block_kernel(
    span,
    heads,
    lens,
    lin_q_far,
    lin_k_far,
    lin_v_far,
    forget_far,
    gain_far,
    soft_q_far,
    soft_k_far,
    soft_v_far,
    lin_out,
    soft_out,
    lin_q,
    lin_k,
    lin_v,
    forget,
    gain,
    soft_q,
    pairs,
    bias,
    local,
    packed,
    paired,
    carries,
    carries_in,
    arrived,
    onward,
    early_in,
    ahead_of,
    across,
    incoming,
    intra,
    queried,
    lin_part,
    soft_part,
    loads,
    stores,
    send_kv,
    recv_kv,
    send_pair,
    recv_pair,
    send_carry,
    recv_carry,
    send_chain,
    recv_chain,
    send_early,
    recv_early,
    send_state,
    recv_state,
):
    f32, bf16 = jnp.float32, jnp.bfloat16
    rows = lin_q.shape[0]
    width = HEAD_DIM
    half = heads // 2
    window = span // 2
    me = lax.axis_index("seq")
    z, x = me // 2, me % 2
    other = me + 1 - 2 * x
    mesh_id = pl.DeviceIdType.MESH

    def load(i):
        src, dst = (
            (soft_k_far, pairs.at[0, 0]),
            (soft_v_far, pairs.at[0, 1]),
            (forget_far, forget),
            (lin_k_far, lin_k),
            (lin_v_far, lin_v),
            (lin_q_far, lin_q),
            (soft_q_far, soft_q),
            (gain_far, gain),
        )[i]
        return pltpu.make_async_copy(src, dst, loads.at[i])

    barrier = pltpu.get_barrier_semaphore()
    near = [(other, True)]
    for d in (2, 4):
        near += [(me + d, me + d < span), (me - d, me >= d)]
    peers = 0
    for target, ok in near:
        peers = peers + jnp.int32(ok)

        @pl.when(ok)
        def _():
            pl.semaphore_signal(barrier, inc=1, device_id={"seq": target}, device_id_type=mesh_id)

    for i in range(8):
        load(i).start()

    def remote(src, dst, send, recv, target):
        return pltpu.make_async_remote_copy(
            src_ref=src,
            dst_ref=dst,
            send_sem=send,
            recv_sem=recv,
            device_id={"seq": target},
            device_id_type=mesh_id,
        )

    def kv_copy(held, slot, ahead):
        return remote(pairs.at[held], pairs.at[slot], send_kv.at[slot], recv_kv.at[slot], me + ahead)

    first_column, second_column = x == 0, x == 1
    kv_sent = (
        (0, 2, 2, me + 2 < span),
        (0, 4, 4, me + 4 < span),
    )
    kv_beside = ((0, 1, 1, first_column),)
    kv_passed = (
        (2, 3, 1, first_column & (me >= 2)),
        (2, 1, -1, second_column & (me >= 2)),
        (4, 3, -1, second_column & (me >= 4)),
    )

    def pair_copy(i):
        return remote(
            packed.at[i], paired.at[i], send_pair.at[i], recv_pair.at[i], other
        )

    def carry_copy():
        return remote(carries, carries_in, send_carry, recv_carry, other)

    def chain_copy(i):
        return remote(onward.at[i], arrived.at[i], send_chain.at[i], recv_chain.at[i], me + 2)

    def early_copy(i):
        return remote(ahead_of.at[i], early_in.at[i], send_early.at[i], recv_early.at[i], me + 2)

    def state_copy(i):
        return remote(
            across.at[i], incoming.at[half * x + i], send_state.at[i], recv_state.at[i], other
        )

    load(0).wait()
    load(1).wait()
    pl.semaphore_wait(barrier, peers)
    for held, slot, ahead, ok in kv_sent:

        @pl.when(ok)
        def _():
            kv_copy(held, slot, ahead).start()

    first = me * rows
    starts = [jnp.int32(0)]
    for i in range(lens.shape[1] - 1):
        starts.append(starts[-1] + lens[0, i])
    where_col = first + lax.broadcasted_iota(jnp.int32, (rows, 1), 0)
    doc_col = jnp.zeros((rows, 1), jnp.int32)
    live_col = jnp.ones((rows, 1), f32)
    last = first + rows - 1
    doc_last = jnp.int32(0)
    live_last = jnp.float32(1.0)
    for s in starts:
        doc_col = jnp.maximum(doc_col, jnp.where(where_col >= s, s, 0))
        live_col = jnp.where((where_col >= s) & (s >= first), 0.0, live_col)
        doc_last = jnp.maximum(doc_last, jnp.where(last >= s, s, 0))
        live_last = jnp.where((last >= s) & (s >= first), 0.0, live_last)

    t_at = lax.broadcasted_iota(jnp.int32, (rows, rows), 0)
    s_at = lax.broadcasted_iota(jnp.int32, (rows, rows), 1)
    tri = (s_at <= t_at).astype(f32)
    load(2).wait()
    logs = forget[...]
    cum = lax.dot_general(
        tri, logs, (((1,), (1,)), ((), ())), precision=lax.Precision.HIGHEST,
        preferred_element_type=f32,
    )
    cum_rows = lax.dot_general(
        logs, tri, (((1,), (1,)), ((), ())), precision=lax.Precision.HIGHEST,
        preferred_element_type=f32,
    )
    end = cum[rows - 1 : rows, :]
    tail_mask = where_col >= doc_last
    tail = jnp.where(tail_mask, jnp.exp(jnp.where(tail_mask, end - cum, 0.0)), 0.0)
    entry = jnp.exp(cum) * live_col
    carries[...] = jnp.broadcast_to(jnp.exp(cum_rows[:, rows - 1 : rows]) * live_last, carries.shape)

    def head(ref, h):
        return ref[:, h * width : (h + 1) * width]

    even = x == 0

    def lanes(h):
        return pl.ds(pl.multiple_of(h * width, width), width)

    carry_copy().start()
    load(3).wait()
    load(4).wait()
    for mine in (False, True):
        for i in range(half):
            h = half * x + i if mine else half * (1 - x) + i
            low, high = tail[:, i : i + 1], tail[:, half + i : half + i + 1]
            scale = jnp.where(even, low, high) if mine else jnp.where(even, high, low)
            keyed = (lin_k[:, lanes(h)].astype(f32) * scale).astype(bf16)
            state = lax.dot_general(
                keyed, lin_v[:, lanes(h)], (((0,), (0,)), ((), ())), preferred_element_type=f32
            )
            if mine:
                local[i] = state
            else:
                packed[i] = state.astype(bf16)
                pair_copy(i).start()
    for held, slot, ahead, ok in kv_beside:

        @pl.when(ok)
        def _():
            kv_copy(held, slot, ahead).start()

    for d in range(1, window + 1):

        @pl.when(me < d)
        def _():
            pairs[d] = jnp.zeros((2, rows, width), bf16)

    mask = (s_at <= t_at) & (first + s_at >= doc_col)
    bias[:, 0:rows] = jnp.where(mask, 0.0, NEGATIVE)
    for d in range(1, window + 1):
        bias[:, d * rows : (d + 1) * rows] = jnp.where(
            first - d * rows + s_at >= doc_col, 0.0, NEGATIVE
        )
    load(5).wait()
    for h in range(heads):
        query = head(lin_q, h)
        diff = cum[:, h : h + 1] - cum_rows[h : h + 1, :]
        decay = jnp.where(mask, jnp.exp(jnp.where(mask, diff, 0.0)), 0.0)
        scores = lax.dot_general(
            query, head(lin_k, h), (((1,), (1,)), ((), ())), preferred_element_type=f32
        )
        intra[h] = jnp.dot(
            (scores * decay).astype(bf16), head(lin_v, h), preferred_element_type=f32
        )
        queried[h] = (query.astype(f32) * entry[:, h : h + 1]).astype(bf16)

    def pass_on(slot_in):
        @pl.when(me >= slot_in)
        def _():
            kv_copy(0, slot_in, slot_in).wait_recv()

        for held, slot, ahead, ok in kv_passed:
            if held == slot_in:

                @pl.when(ok)
                def _():
                    kv_copy(held, slot, ahead).start()

    pass_on(2)
    load(6).wait()
    load(7).wait()

    def softmax():
        key_rows = pairs[:, 0].reshape((window + 1) * rows, width)
        value_rows = pairs[:, 1].reshape((window + 1) * rows, width)
        factor = math.log2(math.e) / math.sqrt(width)
        for h in range(heads):
            scores = lax.dot_general(
                head(soft_q, h), key_rows, (((1,), (1,)), ((), ())), preferred_element_type=f32
            )
            scores = scores + bias[...]
            peak = jnp.max(scores, axis=1, keepdims=True)
            weights = jnp.exp2((scores - peak) * factor)
            total = jnp.sum(weights, axis=1, keepdims=True)
            numer = jnp.dot(weights.astype(bf16), value_rows, preferred_element_type=f32)
            soft_part[:, h * width : (h + 1) * width] = (numer / total).astype(bf16)

    def odd_slots():
        for d in (1, 3):

            @pl.when(me >= d)
            def _():
                kv_copy(0, d, 1).wait_recv()

    carry_copy().wait_recv()

    def parts(i):
        h = half * x + i
        own, far = local[i], paired[i].astype(f32)
        own_carry, far_carry = carries[pl.ds(h, 1), :], carries_in[pl.ds(h, 1), :]
        early, late = jnp.where(even, own, far), jnp.where(even, far, own)
        early_carry = jnp.where(even, own_carry, far_carry)
        late_carry = jnp.where(even, far_carry, own_carry)
        return early, early_carry, late, late_carry

    for i in range(half):
        pair_copy(i).wait_recv()
        early, early_carry, late, late_carry = parts(i)
        pair = late + late_carry * early

        @pl.when(z == 0)
        def _():
            onward[i] = pair.astype(bf16)
            chain_copy(i).start()
            arrived[i] = jnp.zeros((width, width), bf16)

        @pl.when(z == 1)
        def _():
            ahead_of[i] = pair.astype(bf16)
            early_copy(i).start()

        @pl.when(z == 2)
        def _():
            early_copy(i).wait_recv()
            before = early_in[i].astype(f32)
            onward[i] = (pair + (late_carry * early_carry) * before).astype(bf16)
            chain_copy(i).start()

    pass_on(4)
    for i in range(half):
        early, early_carry, late, late_carry = parts(i)

        @pl.when(z > 0)
        def _():
            chain_copy(i).wait_recv()

        entering_even = arrived[i].astype(f32)
        entering_odd = early + early_carry * entering_even

        @pl.when(z == 1)
        def _():
            onward[i] = (late + late_carry * entering_odd).astype(bf16)
            chain_copy(i).start()

        across[i] = jnp.where(even, entering_odd, entering_even).astype(bf16)
        state_copy(i).start()
        incoming[half * x + i] = jnp.where(even, entering_even, entering_odd).astype(bf16)

    odd_slots()
    softmax()
    soft_store = pltpu.make_async_copy(soft_part, soft_out, stores.at[heads])
    soft_store.start()

    def lin_store(h):
        columns = pl.ds(h * width, width)
        return pltpu.make_async_copy(
            lin_part.at[:, columns], lin_out.at[:, columns], stores.at[h]
        )

    for i in range(half):
        state_copy(i).wait_recv()
    for h in range(heads):
        summed = intra[h] + jnp.dot(queried[h], incoming[h], preferred_element_type=f32)
        mean_square = jnp.mean(summed * summed, axis=1, keepdims=True)
        normed = summed * lax.rsqrt(mean_square + 1e-06) * head(gain, h)
        lin_part[:, h * width : (h + 1) * width] = normed.astype(bf16)
        lin_store(h).start()

    carry_copy().wait_send()
    for i in range(half):
        pair_copy(i).wait_send()
        state_copy(i).wait_send()

        @pl.when(me + 2 < span)
        def _():
            chain_copy(i).wait_send()

        @pl.when(z == 1)
        def _():
            early_copy(i).wait_send()

    for held, slot, ahead, ok in kv_sent + kv_beside + kv_passed:

        @pl.when(ok)
        def _():
            kv_copy(held, slot, ahead).wait_send()

    soft_store.wait()
    for h in range(heads):
        lin_store(h).wait()


def results_kernel(lin_in, soft_in, lin_out, soft_out, sems):
    copies = [
        pltpu.make_async_copy(lin_in, lin_out, sems.at[0]),
        pltpu.make_async_copy(soft_in, soft_out, sems.at[1]),
    ]
    for copy in copies:
        copy.start()
    for copy in copies:
        copy.wait()


def in_one_kernel(
    lin_query,
    lin_key,
    lin_value,
    forget_log,
    norm_gain,
    soft_query,
    soft_key,
    soft_value,
    doc_lengths,
):
    span = lax.axis_size("seq")
    rows, columns = lin_query.shape
    heads = columns // HEAD_DIM
    half, window = heads // 2, span // 2
    f32, bf16 = jnp.float32, jnp.bfloat16
    dma = pltpu.SemaphoreType.DMA
    far = pl.BlockSpec(memory_space=pltpu.HBM)
    near = pl.BlockSpec(memory_space=pltpu.VMEM)
    square = (HEAD_DIM, HEAD_DIM)
    shapes = (jax.ShapeDtypeStruct((rows, columns), bf16),) * 2
    lin_out, soft_out = pl.pallas_call(
        functools.partial(block_kernel, span, heads),
        out_shape=shapes,
        in_specs=[pl.BlockSpec(memory_space=pltpu.SMEM)]
        + [far] * 8,
        out_specs=(far, far),
        scratch_shapes=[
            pltpu.VMEM((rows, columns), bf16),
            pltpu.VMEM((rows, columns), bf16),
            pltpu.VMEM((rows, columns), bf16),
            pltpu.VMEM((heads, rows), f32),
            pltpu.VMEM((1, columns), f32),
            pltpu.VMEM((rows, columns), bf16),
            pltpu.VMEM((window + 1, 2, rows, HEAD_DIM), bf16),
            pltpu.VMEM((rows, (window + 1) * rows), f32),
            pltpu.VMEM((half, *square), f32),
            pltpu.VMEM((half, *square), bf16),
            pltpu.VMEM((half, *square), bf16),
            pltpu.VMEM((heads, HEAD_DIM), f32),
            pltpu.VMEM((heads, HEAD_DIM), f32),
            pltpu.VMEM((half, *square), bf16),
            pltpu.VMEM((half, *square), bf16),
            pltpu.VMEM((half, *square), bf16),
            pltpu.VMEM((half, *square), bf16),
            pltpu.VMEM((half, *square), bf16),
            pltpu.VMEM((heads, *square), bf16),
            pltpu.VMEM((heads, rows, HEAD_DIM), f32),
            pltpu.VMEM((heads, rows, HEAD_DIM), bf16),
            pltpu.VMEM((rows, columns), bf16),
            pltpu.VMEM((rows, columns), bf16),
            dma((8,)),
            dma((heads + 1,)),
            dma((window + 1,)),
            dma((window + 1,)),
            dma((half,)),
            dma((half,)),
            dma,
            dma,
            dma((half,)),
            dma((half,)),
            dma((half,)),
            dma((half,)),
            dma((half,)),
            dma((half,)),
        ],
        compiler_params=pltpu.CompilerParams(
            collective_id=0, has_side_effects=True, vmem_limit_bytes=62 << 20
        ),
    )(
        doc_lengths,
        lin_query,
        lin_key,
        lin_value,
        forget_log.T,
        norm_gain.reshape(1, columns),
        soft_query,
        soft_key,
        soft_value,
    )
    return pl.pallas_call(
        results_kernel,
        out_shape=shapes,
        in_specs=[near, near],
        out_specs=(far, far),
        scratch_shapes=[dma((2,))],
    )(lin_out, soft_out)


def solution(mesh):
    placed = (
        P(("rep", "seq"), "sub"),
        P(("rep", "seq"), "sub"),
        P(("rep", "seq"), "sub"),
        P(("rep", "seq"), "sub"),
        P("sub"),
        P(("rep", "seq"), "sub"),
        P(("rep", "seq"), "sub"),
        P(("rep", "seq"), "sub"),
        P("rep", None),
    )
    small = mesh.shape["seq"] == 8
    return jax.shard_map(
        in_one_kernel if small else per_device,
        mesh=mesh,
        in_specs=placed,
        out_specs=(P(("rep", "seq"), "sub"), P(("rep", "seq"), "sub")),
        check_vma=False,
    )
```

```python
import functools
import math

import jax
import jax.numpy as jnp
from jax import lax
from jax.experimental import pallas as pl
from jax.experimental.pallas import tpu as pltpu
from jax.sharding import PartitionSpec as P

HEAD_DIM = 128


NEGATIVE = -1e30


def entering(array, axis, combine, identity):
    size, mine = (lax.axis_size(axis), lax.axis_index(axis))
    everything = jax.tree.map(
        lambda part, kind: lax.all_gather(part.astype(kind), axis),
        array,
        (jnp.bfloat16, jnp.bfloat16),
    )
    start = jax.tree.map(
        lambda part, zero: jnp.broadcast_to(jnp.asarray(zero, part.dtype), part.shape),
        array,
        identity,
    )

    def step(k, before):
        reached = k < mine
        new = combine(
            before, jax.tree.map(lambda part, own: part[k].astype(own.dtype), everything, array)
        )
        return jax.tree.map(lambda a, b: jnp.where(reached, a, b), new, before)

    return lax.fori_loop(0, size, step, start)


def passed_along(block, axis, distance):
    devices = range(lax.axis_size(axis))
    route = [(i - distance, i) for i in devices if i - distance in devices]
    return lax.ppermute(block, axis, route)


def document_ids(lengths_row, where_at):
    starts = jnp.cumsum(lengths_row) - lengths_row
    ids = jnp.sum((starts[None, :] <= where_at[:, None]).astype(jnp.int32), axis=1) - 1
    begins = jnp.any(starts[None, :] == where_at[:, None], axis=1)
    return (ids, begins)


def linear_parts(lin_query, lin_key, lin_value, forget_log, ids, begins):
    rows_here, heads_here = forget_log.shape
    queries = lin_query.reshape(rows_here, heads_here, HEAD_DIM)
    keys = lin_key.reshape(rows_here, heads_here, HEAD_DIM)
    values = lin_value.reshape(rows_here, heads_here, HEAD_DIM)
    cum = jnp.cumsum(forget_log, axis=0)
    live = (jnp.cumsum(begins.astype(jnp.int32)) == 0).astype(jnp.float32)
    order = jnp.arange(rows_here, dtype=jnp.int32)
    mask = (ids[:, None] == ids[None, :]) & (order[None, :] <= order[:, None])
    diff = cum.T[:, :, None] - cum.T[:, None, :]
    decay = jnp.where(mask[None], jnp.exp(jnp.where(mask[None], diff, 0.0)), 0.0)
    scores = jnp.einsum("thd,shd->hts", queries, keys, preferred_element_type=jnp.float32)
    weights = (scores * decay).astype(jnp.bfloat16)
    intra = jnp.einsum("hts,shd->thd", weights, values, preferred_element_type=jnp.float32)
    tail_mask = ids == ids[-1]
    tail = jnp.where(
        tail_mask[:, None], jnp.exp(jnp.where(tail_mask[:, None], cum[-1][None, :] - cum, 0.0)), 0.0
    )
    keyed = (keys * tail[:, :, None]).astype(jnp.bfloat16)
    local_state = jnp.einsum("shd,she->hde", keyed, values, preferred_element_type=jnp.float32)
    block_decay = jnp.exp(cum[-1]) * live[-1]
    queried = (queries * (jnp.exp(cum) * live[:, None])[:, :, None]).astype(jnp.bfloat16)
    return (intra, queried, local_state, block_decay)


def linear_finish(intra, queried, incoming, norm_gain):
    rows_here, heads_here, width = intra.shape
    inter = jnp.einsum(
        "thd,hde->the", queried, incoming.astype(jnp.bfloat16), preferred_element_type=jnp.float32
    )
    summed = intra + inter
    mean_square = jnp.mean(summed * summed, axis=-1, keepdims=True)
    normed = summed * lax.rsqrt(mean_square + 1e-06) * norm_gain.reshape(heads_here, width)
    return normed.reshape(rows_here, heads_here * width).astype(jnp.bfloat16)


def attend(running, queries, key_block, value_block, mask):
    peak, total, accum = running
    width = queries.shape[-1]
    scores = jnp.einsum(
        "tkgd,skd->kgts", queries, key_block, preferred_element_type=jnp.float32
    ) * (1.0 / math.sqrt(width))
    scores = jnp.where(mask, scores, NEGATIVE)
    new_peak = jnp.maximum(peak, jnp.max(scores, axis=-1))
    weights = jnp.where(mask, jnp.exp(scores - new_peak[..., None]), 0.0)
    rescale = jnp.exp(peak - new_peak)
    total = total * rescale + jnp.sum(weights, axis=-1)
    accum = accum * rescale[..., None] + jnp.einsum(
        "kgts,skd->kgtd",
        weights.astype(jnp.bfloat16),
        value_block,
        preferred_element_type=jnp.float32,
    )
    return (new_peak, total, accum)


def start_running(kv_here, group, count):
    return (
        jnp.full((kv_here, group, count), NEGATIVE, jnp.float32),
        jnp.zeros((kv_here, group, count), jnp.float32),
        jnp.zeros((kv_here, group, count, HEAD_DIM), jnp.float32),
    )


def finish_running(running, count, heads_here):
    peak, total, accum = running
    soft = (accum / total[..., None]).astype(jnp.bfloat16)
    return soft.transpose(2, 0, 1, 3).reshape(count, heads_here * HEAD_DIM)


def per_device(
    lin_query,
    lin_key,
    lin_value,
    forget_log,
    norm_gain,
    soft_query,
    soft_key,
    soft_value,
    doc_lengths,
):
    rows_here = lin_query.shape[0]
    seq_count = doc_lengths.shape[0]
    span = lax.axis_size("seq") // seq_count
    position = lax.axis_index("seq")
    rank = position % span
    lengths_row = doc_lengths[0]
    order = jnp.arange(rows_here, dtype=jnp.int32)
    query_where = rank * rows_here + order
    ids, begins = document_ids(lengths_row, query_where)
    intra, queried, local_state, block_decay = linear_parts(
        lin_query, lin_key, lin_value, forget_log, ids, begins
    )

    def combine_states(earlier, later):
        return (earlier[0] * later[0], later[0][:, None, None] * earlier[1] + later[1])

    identity = (jnp.ones_like(block_decay), jnp.zeros_like(local_state))
    scanned = entering((block_decay, local_state), "seq", combine_states, identity)
    lin_out = linear_finish(intra, queried, scanned[1], norm_gain)
    kv_here = soft_key.shape[1] // HEAD_DIM
    heads_here = soft_query.shape[1] // HEAD_DIM
    group = heads_here // kv_here
    queries = soft_query.reshape(rows_here, kv_here, group, HEAD_DIM)

    def piece_mask(start, count):
        key_where = start + jnp.arange(count, dtype=jnp.int32)
        source_ids, unused = document_ids(lengths_row, key_where)
        return (ids[:, None] == source_ids[None, :]) & (key_where[None, :] <= query_where[:, None])

    def attend_piece(running, key_piece, value_piece, start):
        count = key_piece.shape[0]
        key_block = key_piece.reshape(count, kv_here, HEAD_DIM)
        value_block = value_piece.reshape(count, kv_here, HEAD_DIM)
        return attend(running, queries, key_block, value_block, piece_mask(start, count))

    own_pair = jnp.stack([soft_key, soft_value])
    running = attend_piece(
        start_running(kv_here, group, rows_here), soft_key, soft_value, rank * rows_here
    )

    def visit_cycle(turn, state):
        moving, inner_state = state
        moving = passed_along(moving, "seq", 1)
        source = rank - turn - 1
        inner_state = lax.cond(
            source >= 0,
            lambda inner: attend_piece(inner, moving[0], moving[1], source * rows_here),
            lambda inner: inner,
            inner_state,
        )
        return (moving, inner_state)

    unused_pair, running = lax.fori_loop(0, span - 1, visit_cycle, (own_pair, running))
    soft_out = finish_running(running, rows_here, heads_here)
    return (lin_out, soft_out)


def block_kernel(
    span,
    heads,
    lens,
    lin_q_far,
    lin_k_far,
    lin_v_far,
    forget_far,
    soft_q_far,
    soft_k_far,
    soft_v_far,
    intra_out,
    queried_out,
    incoming,
    soft_out,
    lin_q,
    lin_k,
    lin_v,
    forget,
    soft_q,
    pairs,
    bias,
    local,
    packed,
    paired,
    carries,
    carries_in,
    arrived,
    onward,
    early_in,
    ahead_of,
    across,
    entered,
    intra,
    queried,
    soft_part,
    loads,
    stores,
    send_kv,
    recv_kv,
    send_pair,
    recv_pair,
    send_carry,
    recv_carry,
    send_chain,
    recv_chain,
    send_early,
    recv_early,
    send_state,
    recv_state,
):
    f32, bf16 = jnp.float32, jnp.bfloat16
    rows = lin_q.shape[0]
    width = HEAD_DIM
    half = heads // 2
    window = span // 2
    me = lax.axis_index("seq")
    z, x = me // 2, me % 2
    other = me + 1 - 2 * x
    mesh_id = pl.DeviceIdType.MESH

    def load(i):
        src, dst = (
            (soft_k_far, pairs.at[0, 0]),
            (soft_v_far, pairs.at[0, 1]),
            (forget_far, forget),
            (lin_k_far, lin_k),
            (lin_v_far, lin_v),
            (lin_q_far, lin_q),
            (soft_q_far, soft_q),
        )[i]
        return pltpu.make_async_copy(src, dst, loads.at[i])

    barrier = pltpu.get_barrier_semaphore()
    near = [(other, True)]
    for d in (2, 4):
        near += [(me + d, me + d < span), (me - d, me >= d)]
    peers = 0
    for target, ok in near:
        peers = peers + jnp.int32(ok)

        @pl.when(ok)
        def _():
            pl.semaphore_signal(barrier, inc=1, device_id={"seq": target}, device_id_type=mesh_id)

    for i in range(7):
        load(i).start()

    def remote(src, dst, send, recv, target):
        return pltpu.make_async_remote_copy(
            src_ref=src,
            dst_ref=dst,
            send_sem=send,
            recv_sem=recv,
            device_id={"seq": target},
            device_id_type=mesh_id,
        )

    def kv_copy(held, slot, ahead):
        return remote(pairs.at[held], pairs.at[slot], send_kv.at[slot], recv_kv.at[slot], me + ahead)

    first_column, second_column = x == 0, x == 1
    kv_sent = (
        (0, 2, 2, me + 2 < span),
        (0, 4, 4, me + 4 < span),
    )
    kv_beside = ((0, 1, 1, first_column),)
    kv_passed = (
        (2, 3, 1, first_column & (me >= 2)),
        (2, 1, -1, second_column & (me >= 2)),
        (4, 3, -1, second_column & (me >= 4)),
    )

    def pair_copy(i):
        return remote(
            packed.at[i], paired.at[i], send_pair.at[i], recv_pair.at[i], other
        )

    def carry_copy():
        return remote(carries, carries_in, send_carry, recv_carry, other)

    def chain_copy(i):
        return remote(onward.at[i], arrived.at[i], send_chain.at[i], recv_chain.at[i], me + 2)

    def early_copy(i):
        return remote(ahead_of.at[i], early_in.at[i], send_early.at[i], recv_early.at[i], me + 2)

    def state_copy(i):
        return remote(
            across.at[i], incoming.at[half * x + i], send_state.at[i], recv_state.at[i], other
        )

    load(0).wait()
    load(1).wait()
    pl.semaphore_wait(barrier, peers)
    for held, slot, ahead, ok in kv_sent:

        @pl.when(ok)
        def _():
            kv_copy(held, slot, ahead).start()

    first = me * rows
    starts = [jnp.int32(0)]
    for i in range(lens.shape[1] - 1):
        starts.append(starts[-1] + lens[0, i])
    where_col = first + lax.broadcasted_iota(jnp.int32, (rows, 1), 0)
    doc_col = jnp.zeros((rows, 1), jnp.int32)
    live_col = jnp.ones((rows, 1), f32)
    last = first + rows - 1
    doc_last = jnp.int32(0)
    live_last = jnp.float32(1.0)
    for s in starts:
        doc_col = jnp.maximum(doc_col, jnp.where(where_col >= s, s, 0))
        live_col = jnp.where((where_col >= s) & (s >= first), 0.0, live_col)
        doc_last = jnp.maximum(doc_last, jnp.where(last >= s, s, 0))
        live_last = jnp.where((last >= s) & (s >= first), 0.0, live_last)

    t_at = lax.broadcasted_iota(jnp.int32, (rows, rows), 0)
    s_at = lax.broadcasted_iota(jnp.int32, (rows, rows), 1)
    tri = (s_at <= t_at).astype(f32)
    load(2).wait()
    logs = forget[...]
    cum = lax.dot_general(
        tri, logs, (((1,), (1,)), ((), ())), precision=lax.Precision.HIGHEST,
        preferred_element_type=f32,
    )
    cum_rows = lax.dot_general(
        logs, tri, (((1,), (1,)), ((), ())), precision=lax.Precision.HIGHEST,
        preferred_element_type=f32,
    )
    end = cum[rows - 1 : rows, :]
    tail_mask = where_col >= doc_last
    tail = jnp.where(tail_mask, jnp.exp(jnp.where(tail_mask, end - cum, 0.0)), 0.0)
    entry = jnp.exp(cum) * live_col
    carries[...] = jnp.broadcast_to(jnp.exp(cum_rows[:, rows - 1 : rows]) * live_last, carries.shape)

    def head(ref, h):
        return ref[:, h * width : (h + 1) * width]

    even = x == 0

    def lanes(h):
        return pl.ds(pl.multiple_of(h * width, width), width)

    carry_copy().start()
    load(3).wait()
    load(4).wait()
    for mine in (False, True):
        for i in range(half):
            h = half * x + i if mine else half * (1 - x) + i
            low, high = tail[:, i : i + 1], tail[:, half + i : half + i + 1]
            scale = jnp.where(even, low, high) if mine else jnp.where(even, high, low)
            keyed = (lin_k[:, lanes(h)].astype(f32) * scale).astype(bf16)
            state = lax.dot_general(
                keyed, lin_v[:, lanes(h)], (((0,), (0,)), ((), ())), preferred_element_type=f32
            )
            if mine:
                local[i] = state
            else:
                packed[i] = state.astype(bf16)
                pair_copy(i).start()
    for held, slot, ahead, ok in kv_beside:

        @pl.when(ok)
        def _():
            kv_copy(held, slot, ahead).start()

    for d in range(1, window + 1):

        @pl.when(me < d)
        def _():
            pairs[d] = jnp.zeros((2, rows, width), bf16)

    mask = (s_at <= t_at) & (first + s_at >= doc_col)
    bias[:, 0:rows] = jnp.where(mask, 0.0, NEGATIVE)
    for d in range(1, window + 1):
        bias[:, d * rows : (d + 1) * rows] = jnp.where(
            first - d * rows + s_at >= doc_col, 0.0, NEGATIVE
        )
    load(5).wait()
    for h in range(heads):
        query = head(lin_q, h)
        diff = cum[:, h : h + 1] - cum_rows[h : h + 1, :]
        decay = jnp.where(mask, jnp.exp(jnp.where(mask, diff, 0.0)), 0.0)
        scores = lax.dot_general(
            query, head(lin_k, h), (((1,), (1,)), ((), ())), preferred_element_type=f32
        )
        intra[h] = jnp.dot(
            (scores * decay).astype(bf16), head(lin_v, h), preferred_element_type=f32
        )
        queried[h] = (query.astype(f32) * entry[:, h : h + 1]).astype(bf16)

    def part_store(i):
        src, dst = ((intra, intra_out), (queried, queried_out), (soft_part, soft_out))[i]
        return pltpu.make_async_copy(src, dst, stores.at[i])

    def entered_store(i):
        return pltpu.make_async_copy(entered.at[i], incoming.at[half * x + i], stores.at[3 + i])

    part_store(0).start()
    part_store(1).start()

    def pass_on(slot_in):
        @pl.when(me >= slot_in)
        def _():
            kv_copy(0, slot_in, slot_in).wait_recv()

        for held, slot, ahead, ok in kv_passed:
            if held == slot_in:

                @pl.when(ok)
                def _():
                    kv_copy(held, slot, ahead).start()

    pass_on(2)
    load(6).wait()

    def softmax():
        key_rows = pairs[:, 0].reshape((window + 1) * rows, width)
        value_rows = pairs[:, 1].reshape((window + 1) * rows, width)
        factor = math.log2(math.e) / math.sqrt(width)
        for h in range(heads):
            scores = lax.dot_general(
                head(soft_q, h), key_rows, (((1,), (1,)), ((), ())), preferred_element_type=f32
            )
            scores = scores + bias[...]
            peak = jnp.max(scores, axis=1, keepdims=True)
            weights = jnp.exp2((scores - peak) * factor)
            total = jnp.sum(weights, axis=1, keepdims=True)
            numer = jnp.dot(weights.astype(bf16), value_rows, preferred_element_type=f32)
            soft_part[:, h * width : (h + 1) * width] = (numer / total).astype(bf16)

    def odd_slots():
        for d in (1, 3):

            @pl.when(me >= d)
            def _():
                kv_copy(0, d, 1).wait_recv()

    carry_copy().wait_recv()

    def parts(i):
        h = half * x + i
        own, far = local[i], paired[i].astype(f32)
        own_carry, far_carry = carries[pl.ds(h, 1), :], carries_in[pl.ds(h, 1), :]
        early, late = jnp.where(even, own, far), jnp.where(even, far, own)
        early_carry = jnp.where(even, own_carry, far_carry)
        late_carry = jnp.where(even, far_carry, own_carry)
        return early, early_carry, late, late_carry

    for i in range(half):
        pair_copy(i).wait_recv()
        early, early_carry, late, late_carry = parts(i)
        pair = late + late_carry * early

        @pl.when(z == 0)
        def _():
            onward[i] = pair.astype(bf16)
            chain_copy(i).start()
            arrived[i] = jnp.zeros((width, width), bf16)

        @pl.when(z == 1)
        def _():
            ahead_of[i] = pair.astype(bf16)
            early_copy(i).start()

        @pl.when(z == 2)
        def _():
            early_copy(i).wait_recv()
            before = early_in[i].astype(f32)
            onward[i] = (pair + (late_carry * early_carry) * before).astype(bf16)
            chain_copy(i).start()

    pass_on(4)
    for i in range(half):
        early, early_carry, late, late_carry = parts(i)

        @pl.when(z > 0)
        def _():
            chain_copy(i).wait_recv()

        entering_even = arrived[i].astype(f32)
        entering_odd = early + early_carry * entering_even

        @pl.when(z == 1)
        def _():
            onward[i] = (late + late_carry * entering_odd).astype(bf16)
            chain_copy(i).start()

        across[i] = jnp.where(even, entering_odd, entering_even).astype(bf16)
        state_copy(i).start()
        entered[i] = jnp.where(even, entering_even, entering_odd).astype(bf16)
        entered_store(i).start()

    odd_slots()
    softmax()
    part_store(2).start()
    for i in range(half):
        state_copy(i).wait_recv()
    carry_copy().wait_send()
    for i in range(half):
        pair_copy(i).wait_send()
        state_copy(i).wait_send()

        @pl.when(me + 2 < span)
        def _():
            chain_copy(i).wait_send()

        @pl.when(z == 1)
        def _():
            early_copy(i).wait_send()

    for held, slot, ahead, ok in kv_sent + kv_beside + kv_passed:

        @pl.when(ok)
        def _():
            kv_copy(held, slot, ahead).wait_send()

    for i in range(3):
        part_store(i).wait()
    for i in range(half):
        entered_store(i).wait()


def finish_kernel(
    heads, intra_far, queried_far, incoming_far, soft_far, gain, lin_out, soft_out,
    intra, queried, incoming, soft, lin, loads, stores,
):
    width = HEAD_DIM

    def load(i, h):
        src, dst = ((intra_far, intra), (queried_far, queried), (incoming_far, incoming))[i]
        return pltpu.make_async_copy(src.at[h], dst.at[h], loads.at[3 * h + i])

    def lin_store(h):
        columns = pl.ds(h * width, width)
        return pltpu.make_async_copy(lin.at[:, columns], lin_out.at[:, columns], stores.at[h])

    soft_load = pltpu.make_async_copy(soft_far, soft, loads.at[3 * heads])
    soft_store = pltpu.make_async_copy(soft, soft_out, stores.at[heads])
    soft_load.start()
    for h in range(heads):
        for i in range(3):
            load(i, h).start()
    soft_load.wait()
    soft_store.start()
    for h in range(heads):
        for i in range(3):
            load(i, h).wait()
        summed = intra[h] + jnp.dot(queried[h], incoming[h], preferred_element_type=jnp.float32)
        mean_square = jnp.mean(summed * summed, axis=1, keepdims=True)
        columns = slice(h * width, (h + 1) * width)
        normed = summed * lax.rsqrt(mean_square + 1e-06) * gain[:, columns]
        lin[:, columns] = normed.astype(jnp.bfloat16)
        lin_store(h).start()
    soft_store.wait()
    for h in range(heads):
        lin_store(h).wait()


def in_one_kernel(
    lin_query,
    lin_key,
    lin_value,
    forget_log,
    norm_gain,
    soft_query,
    soft_key,
    soft_value,
    doc_lengths,
):
    span = lax.axis_size("seq")
    rows, columns = lin_query.shape
    heads = columns // HEAD_DIM
    half, window = heads // 2, span // 2
    f32, bf16 = jnp.float32, jnp.bfloat16
    dma = pltpu.SemaphoreType.DMA
    far = pl.BlockSpec(memory_space=pltpu.HBM)
    near = pl.BlockSpec(memory_space=pltpu.VMEM)
    square = (HEAD_DIM, HEAD_DIM)
    shape = jax.ShapeDtypeStruct
    states = (heads, *square)
    parts = (shape(states, f32), shape(states, bf16), shape(states, bf16), shape((rows, columns), bf16))
    parts = pl.pallas_call(
        functools.partial(block_kernel, span, heads),
        out_shape=parts,
        in_specs=[pl.BlockSpec(memory_space=pltpu.SMEM)]
        + [far] * 7,
        out_specs=(far,) * 4,
        scratch_shapes=[
            pltpu.VMEM((rows, columns), bf16),
            pltpu.VMEM((rows, columns), bf16),
            pltpu.VMEM((rows, columns), bf16),
            pltpu.VMEM((heads, rows), f32),
            pltpu.VMEM((rows, columns), bf16),
            pltpu.VMEM((window + 1, 2, rows, HEAD_DIM), bf16),
            pltpu.VMEM((rows, (window + 1) * rows), f32),
            pltpu.VMEM((half, *square), f32),
            pltpu.VMEM((half, *square), bf16),
            pltpu.VMEM((half, *square), bf16),
            pltpu.VMEM((heads, HEAD_DIM), f32),
            pltpu.VMEM((heads, HEAD_DIM), f32),
            pltpu.VMEM((half, *square), bf16),
            pltpu.VMEM((half, *square), bf16),
            pltpu.VMEM((half, *square), bf16),
            pltpu.VMEM((half, *square), bf16),
            pltpu.VMEM((half, *square), bf16),
            pltpu.VMEM((half, *square), bf16),
            pltpu.VMEM((heads, rows, HEAD_DIM), f32),
            pltpu.VMEM((heads, rows, HEAD_DIM), bf16),
            pltpu.VMEM((rows, columns), bf16),
            dma((7,)),
            dma((3 + half,)),
            dma((window + 1,)),
            dma((window + 1,)),
            dma((half,)),
            dma((half,)),
            dma,
            dma,
            dma((half,)),
            dma((half,)),
            dma((half,)),
            dma((half,)),
            dma((half,)),
            dma((half,)),
        ],
        compiler_params=pltpu.CompilerParams(
            collective_id=0, has_side_effects=True, vmem_limit_bytes=62 << 20
        ),
    )(
        doc_lengths,
        lin_query,
        lin_key,
        lin_value,
        forget_log.T,
        soft_query,
        soft_key,
        soft_value,
    )
    return pl.pallas_call(
        functools.partial(finish_kernel, heads),
        out_shape=(shape((rows, columns), bf16),) * 2,
        in_specs=[far] * 4 + [near],
        out_specs=(far, far),
        scratch_shapes=[
            pltpu.VMEM(states, f32),
            pltpu.VMEM(states, bf16),
            pltpu.VMEM(states, bf16),
            pltpu.VMEM((rows, columns), bf16),
            pltpu.VMEM((rows, columns), bf16),
            dma((3 * heads + 1,)),
            dma((heads + 1,)),
        ],
        compiler_params=pltpu.CompilerParams(vmem_limit_bytes=62 << 20),
    )(*parts, norm_gain.reshape(1, columns))


def solution(mesh):
    placed = (
        P(("rep", "seq"), "sub"),
        P(("rep", "seq"), "sub"),
        P(("rep", "seq"), "sub"),
        P(("rep", "seq"), "sub"),
        P("sub"),
        P(("rep", "seq"), "sub"),
        P(("rep", "seq"), "sub"),
        P(("rep", "seq"), "sub"),
        P("rep", None),
    )
    small = mesh.shape["seq"] == 8
    return jax.shard_map(
        in_one_kernel if small else per_device,
        mesh=mesh,
        in_specs=placed,
        out_specs=(P(("rep", "seq"), "sub"), P(("rep", "seq"), "sub")),
        check_vma=False,
    )
```
